512 devices in a mesh: rows: 64 (over y_hi, z, core), cols: 8 (over y_lo, x).
Axes of the slice: x: 4, y: 8 (y_hi: 4, y_lo: 2; y = y_hi * 2 + y_lo), z: 8, core: 2. Of those that a mesh axis runs over, the one named last changes fastest.
Arguments:
- residual: bfloat16 [2, 8192, 8192], P(None, 'rows', 'cols'), may hold values from -6 to 6
- field_slopes: bfloat16 [4, 8192, 8192], P(None, 'rows', 'cols'), may hold values from -6 to 6
- source_tile: int32 [2, 8192, 64], P(None, 'rows', 'cols'), may hold values from 0 to 7
- row_shift: int32 [2, 8192, 64], P(None, 'rows', 'cols'), may hold values from -8 to 8
- pixel_shift: int32 [2, 8192, 64], P(None, 'rows', 'cols'), may hold values from -2 to 2
- fraction: float32 [2, 8192, 64], P(None, 'rows', 'cols'), may hold values from 0 to 1
Outputs:
- potential_step: float32 [8192, 8192], P('rows', 'cols')
The draws below stay inside these ranges and needn't reach their ends.
Inputs may be any that keep to these rules, and one draw needn't show every extreme that they name: `source_tile`: a tile number inside the group of 8 tiles that holds the destination tile.
All inputs are finite; a program needn't handle non-finite values.
Results may differ from the reference program's by a relative error of at most 0.0003.
Values may be sent and summed in bfloat16 or wider, within the bound.
A program may use at most 64 MiB of HBM per device.

```python
import math
from functools import partial
import jax
import jax.numpy as jnp
from jax import lax

N = 8192
TILE = 128
PAIRS = 2
HALO = 8
SHIFT = 2
TILES = 64
N_ROWS = 64
N_COLS = 8


def set_ends(entries, stream_key, smallest, high):
    longest = entries.shape.index(max(entries.shape))
    spots = []
    for shift in (0, 1):
        where = [jax.random.randint(jax.random.fold_in(stream_key, axis), (), 0, length) for axis, length in enumerate(entries.shape)]
        where[longest] = (where[longest] + shift) % entries.shape[longest]
        spots.append(tuple(where))
    return entries.at[spots[0]].set(smallest).at[spots[1]].set(high)


def levels(own_key, dims, shards, low, high):
    def one(position, blocks):
        steps = jax.random.uniform(jax.random.fold_in(jax.random.fold_in(own_key, 6), position), (blocks,), jnp.float32, low / len(shards), high / len(shards))
        return jnp.repeat(jnp.exp(steps), dims[position] // blocks).reshape((-1,) + (1,) * (len(dims) - position - 1))

    factor_of = one(*shards[0])
    for cut in shards[1:]:
        factor_of = factor_of * one(*cut)
    return factor_of


def bell_draw(rng, dims, scale, bound, cuts=(), kind=jnp.bfloat16):
    values = jax.random.normal(rng, dims, jnp.float32) * scale
    if len(cuts) > 0:
        values = levels(rng, dims, cuts, -0.22, 0.18) * values
    return jnp.clip(values, min=-bound, max=bound).astype(kind)


def setup_inputs(seed: int = 0) -> dict:
    keys = jax.random.split(jax.random.key(seed), 7)
    return {
        "residual": bell_draw(keys[0], (2, N, N), 1.0, 6.0, ((1, 64), (2, 8))),
        "field_slopes": bell_draw(keys[1], (4, N, N), 1.0, 6.0, ((1, 64), (2, 8))),
        "source_tile": set_ends(jax.random.randint(keys[2], (PAIRS, N, TILES), 0, N // N_COLS // TILE), jax.random.fold_in(keys[2], 1), 0, (N // N_COLS // TILE) - 1).astype(jnp.int32),
        "row_shift": set_ends(jax.random.randint(keys[3], (PAIRS, N, TILES), -HALO, HALO + 1), jax.random.fold_in(keys[3], 1), -HALO, HALO).astype(jnp.int32),
        "pixel_shift": set_ends(jax.random.randint(keys[4], (PAIRS, N, TILES), -SHIFT, SHIFT + 1), jax.random.fold_in(keys[4], 1), -SHIFT, SHIFT).astype(jnp.int32),
        "fraction": jnp.clip(1.0 * jax.random.uniform(keys[5], (PAIRS, N, TILES), jnp.float32) ** levels(keys[5], (PAIRS, N, TILES), ((1, 64), (2, 8)), -0.2, 0.2), 0.0, 1.0),
    }


local_weight = 0.5


def signed_wave(counter):
    middle = N // 2
    shifted = jnp.where(counter > middle, counter - N, counter)
    shifted = jnp.where(counter == middle, 0, shifted)
    return shifted.astype(jnp.float32) * (2.0 * math.pi / N)


def sample_tile(picked, spots):
    inside = (spots >= 0) & (spots < TILE)
    clipped = jnp.clip(spots, 0, TILE - 1)
    values = jnp.take_along_axis(picked, jnp.broadcast_to(clipped[None], picked.shape), axis=4)
    return jnp.where(inside[None], values, 0.0)


def band_flow(band_index, padded, field_slopes, source_tile, row_shift, pixel_shift, fraction):
    rows_dev = N // N_ROWS
    tiles_all = N // TILE
    tiles_dev = N // N_COLS // TILE
    first_row = band_index * rows_dev
    tile_rows = lax.dynamic_slice_in_dim(padded, first_row, rows_dev + 2 * HALO, 1)
    tile_rows = tile_rows.reshape(2, (rows_dev + 2 * HALO) * tiles_all, TILE)
    sources = lax.dynamic_slice_in_dim(source_tile, first_row, rows_dev, 1)
    shifts = lax.dynamic_slice_in_dim(row_shift, first_row, rows_dev, 1)
    offsets = lax.dynamic_slice_in_dim(pixel_shift, first_row, rows_dev, 1)
    blends = lax.dynamic_slice_in_dim(fraction, first_row, rows_dev, 1)
    row_index = jnp.arange(rows_dev, dtype=jnp.int32)[None, :, None]
    tile_index = jnp.arange(tiles_all, dtype=jnp.int32)[None, None, :]
    chosen = tile_index // tiles_dev * tiles_dev + sources
    flat_index = ((row_index + HALO + shifts) * tiles_all + chosen).astype(jnp.int32)
    picked = jnp.take(tile_rows, flat_index.reshape(-1), axis=1)
    picked = picked.reshape(2, PAIRS, rows_dev, tiles_all, TILE).astype(jnp.float32)
    spots = jnp.arange(TILE, dtype=jnp.int32) + offsets[..., None]
    lower = sample_tile(picked, spots)
    upper = sample_tile(picked, spots + 1)
    blend_four = blends[None, :, :, :, None]
    pulled = jnp.sum((1.0 - blend_four) * lower + blend_four * upper, axis=1).reshape(2, rows_dev, N)
    slopes = lax.dynamic_slice_in_dim(field_slopes, first_row, rows_dev, 1).astype(jnp.float32)
    flow_across = -(pulled[0] * slopes[0] + pulled[1] * slopes[1])
    downward_flow = -(pulled[0] * slopes[2] + pulled[1] * slopes[3])
    return jnp.stack([flow_across, downward_flow])


def reference(residual, field_slopes, source_tile, row_shift, pixel_shift, fraction):
    padded = jnp.pad(residual, ((0, 0), (HALO, HALO), (0, 0)))
    bands = jnp.arange(N_ROWS, dtype=jnp.int32)
    patch_worker = partial(band_flow, padded=padded, field_slopes=field_slopes, source_tile=source_tile,
                     row_shift=row_shift, pixel_shift=pixel_shift, fraction=fraction)
    flow_maps = lax.map(patch_worker, bands)
    flow_maps = jnp.transpose(flow_maps, (1, 0, 2, 3)).reshape(2, N, N)
    spectrum_across = jnp.fft.rfft2(flow_maps[0])
    spectrum_down = jnp.fft.rfft2(flow_maps[1])
    wave_rows = signed_wave(jnp.arange(N, dtype=jnp.int32))[:, None]
    wave_cols = signed_wave(jnp.arange(N // 2 + 1, dtype=jnp.int32))[None, :]
    floored_wavenumber = 8.0 * math.pi / N
    weight = local_weight + 1.0 / (wave_rows * wave_rows + wave_cols * wave_cols + floored_wavenumber * floored_wavenumber)
    combined = (weight * wave_cols) * spectrum_across + (weight * wave_rows) * spectrum_down
    return jnp.fft.irfft2(-1j * combined, s=(N, N)).astype(jnp.float32)
```

```python
import functools
import math

import jax
import jax.numpy as jnp
import ml_dtypes
import numpy as np
from jax import lax
from jax.experimental import pallas as pl
from jax.experimental.pallas import tpu as pltpu
from jax.sharding import PartitionSpec as P

N = 8192
TILE = 128
HALO = 8
SHIFT = 2
LOCAL_WEIGHT = 0.5
FLOOR = 8.0 * math.pi / N

F32 = jnp.float32
BF16 = jnp.bfloat16


def split_table(x):
    hi = x.astype(ml_dtypes.bfloat16)
    lo = (x - hi.astype(np.float64)).astype(ml_dtypes.bfloat16)
    return hi, lo


def cs(angle):
    return np.cos(angle), np.sin(angle)


@functools.lru_cache(maxsize=None)
def tables():
    two_pi = 2.0 * np.pi
    t = {}
    p = np.arange(64)[None, :]
    kk = np.arange(32)[:, None]
    c, s = cs(two_pi * ((p * kk) % 64) / 64)
    d1 = np.concatenate([c, -s], 0)
    d1[32] = (-1.0) ** np.arange(64)
    t["d1"] = split_table(d1)
    d4 = np.concatenate([2 * c, -2 * s], 0).T.copy()
    d4[:, 0] = 1.0
    d4[:, 32] = (-1.0) ** np.arange(64)
    t["d4"] = split_table(d4 / (N * N))
    q = np.arange(128)[None, :]
    c, s = cs(two_pi * (kk * q) / N)
    t["tw1"] = np.stack([c, s]).astype(np.float32)
    l = np.arange(128)[:, None]
    c, s = cs(two_pi * ((l * q) % 128) / 128)
    f2 = np.block([[c, s], [-s, c]])
    t["f2"] = split_table(f2)
    t["f4"] = split_table(np.block([[c, s], [-s, c]]))
    c32, s32 = cs(two_pi * ((q * (32 + 64 * l)) % N) / N)
    low = l < 64
    alt = np.broadcast_to((-1.0) ** q, (1, 128))
    m0 = np.zeros((256, 256))
    m0[:128, :128] = np.where(low, c, 0.0)
    m0[128:, :128] = np.where(low, -s, 0.0)
    m0[128:129, :128] = alt
    m0[:128, 128:] = np.where(low, 0.0, c32)
    m0[128:, 128:] = np.where(low, 0.0, -s32)
    t["m0"] = split_table(m0)
    mi = 2.0 * m0
    mi[0] *= 0.5
    mi[128] *= 0.5
    t["m0i"] = split_table(mi)
    r = np.arange(64)[:, None]
    m = np.arange(64)[None, :]
    c, s = cs(two_pi * ((r * m) % 64) / 64)
    e_re = np.concatenate([c, s], 0)
    e_im = np.concatenate([-s, c], 0)
    t["e"] = split_table(np.concatenate([e_re, e_im, -e_im, e_re], 1))
    t["e4"] = split_table(np.block([[c, -s], [s, c]]))
    q2 = np.arange(128)[:, None]
    mm = np.concatenate([np.arange(64), np.arange(64)])[None, :]
    c, s = cs(two_pi * (q2 * mm) / N)
    t["tw2"] = np.stack([c, s]).astype(np.float32)
    n = np.arange(128)[:, None]
    c, s = cs(two_pi * ((n * q2.T) % 128) / 128)
    t["w2"] = split_table(np.concatenate([c, -s], 1))
    t["w3"] = split_table(np.block([[s, -c], [c, s]]))
    a = mm + 64 * n
    signed = np.where(a > N // 2, a - N, np.where(a == N // 2, 0, a))
    t["ka"] = (signed * (two_pi / N)).astype(np.float32)
    return t


def split(x):
    hi = x.astype(BF16)
    return hi, (x - hi.astype(F32)).astype(BF16)


def dot(a, b, transposed=False):
    dims = (((1,), (1 if transposed else 0,)), ((), ()))
    return lax.dot_general(a, b, dims, preferred_element_type=F32)


def dot3(a, b, transposed=False):
    (ah, al), (bh, bl) = a, b
    return dot(ah, bh, transposed) + (dot(ah, bl, transposed) + dot(al, bh, transposed))


def pair(ref):
    return ref[0], ref[1]


def pull_kernel(x, before, after, slopes, tile, rshift, pshift, frac, o, padded, cols):
    padded[:, 0:HALO, :] = before[...].astype(F32)
    padded[:, HALO : HALO + 128, :] = x[...].astype(F32)
    padded[:, HALO + 128 :, :] = after[...].astype(F32)
    flat = lambda ref: ref[...].reshape(16, 128)
    lane = lax.broadcasted_iota(jnp.int32, (16, 128), 1)
    index = flat(tile) * 32 + (lax.rem(lane, 16) + HALO) + flat(rshift)
    ps = flat(pshift)
    f = flat(frac)
    rows = [index.astype(F32)]
    for off in range(-SHIFT, SHIFT + 2):
        w = jnp.where(ps == off, 1.0 - f, 0.0) + jnp.where(ps + 1 == off, f, 0.0)
        rows.append(w)
    rows.append(jnp.zeros((16, 128), F32))
    cols[...] = jnp.concatenate(rows, 0).T

    spot = lax.broadcasted_iota(jnp.int32, (16, 256), 1).astype(F32)
    lane_j = lax.broadcasted_iota(jnp.int32, (16, 128), 1)

    def block(b, _):
        r0 = pl.multiple_of(b * 16, 16)
        window = [
            jnp.concatenate(
                [padded[p, pl.ds(r0, 32), u * 128 : (u + 1) * 128] for u in range(8)], 0
            )
            for p in range(2)
        ]
        window = jnp.concatenate(window, 1).astype(BF16)
        tab = cols[pl.ds(r0, 16), :]
        hot = jnp.concatenate(
            [jnp.where(tab[:, kt : kt + 1] == spot, 1.0, 0.0) for kt in range(16)], 0
        ).astype(BF16)
        picked = dot(hot, window)
        for t in range(8):
            got = []
            for p in range(2):
                total = None
                for oi in range(6):
                    off = oi - SHIFT
                    z = None
                    for k in range(2):
                        kt = k * 8 + t
                        w = tab[:, 16 * (oi + 1) + kt : 16 * (oi + 1) + kt + 1]
                        part = w * picked[kt * 16 : kt * 16 + 16, p * 128 : p * 128 + 128]
                        z = part if z is None else z + part
                    if off != 0:
                        z = pltpu.roll(z, (-off) % 128, 1)
                        keep = lane_j >= -off if off < 0 else lane_j < 128 - off
                        z = jnp.where(keep, z, 0.0)
                    total = z if total is None else total + z
                got.append(total)
            s = [slopes[i, pl.ds(r0, 16), t * 128 : (t + 1) * 128].astype(F32) for i in range(4)]
            o[b, t, 0] = -(got[0] * s[0] + got[1] * s[1])
            o[b, t, 1] = -(got[0] * s[2] + got[1] * s[3])
        return 0

    lax.fori_loop(0, 8, block, 0)


def column_kernel(g, d1, tw, f2, m0, o, ure, uim):
    cos, sin = tw[0], tw[1]
    for grp in range(8):
        x = jnp.concatenate([g[pl.ds(grp * 4 + j, 64, stride=32), :] for j in range(4)], 1)
        v = dot3(pair(d1), split(x))
        for j in range(4):
            re = v[:32, j * 128 : (j + 1) * 128]
            im = v[32:, j * 128 : (j + 1) * 128]
            ure[pl.ds(grp * 4 + j, 32, stride=32), :] = re * cos + im * sin
            uim[pl.ds(grp * 4 + j, 32, stride=32), :] = im * cos - re * sin
    lane = lax.broadcasted_iota(jnp.int32, (256, 128), 1)
    for kg in range(4):
        rows = slice(kg * 256, (kg + 1) * 256)
        rhs = split(jnp.concatenate([ure[rows, :], uim[rows, :]], 1))
        out = dot3(pair(f2), rhs, True)
        for h in range(2):
            part = out[:, h * 128 : (h + 1) * 128]
            if kg == 0 and h == 0:
                special = dot3(pair(m0), (rhs[0][:128], rhs[1][:128]), True)
                part = jnp.where(lane < 32, special, part)
            for ri in range(2):
                o[pl.ds(kg * 4 + ri * 2 + h, 128, stride=16), :] = part[ri * 128 : (ri + 1) * 128]


def row_kernel(kb, x, e, tw, w2, ka_ref, w3, e4, o, uh, ul, sh, sl, yh, yl):
    for c in range(8):
        cos = jnp.concatenate([tw[0, c * 16 : c * 16 + 16, :]] * 8, 0)
        sin = jnp.concatenate([tw[1, c * 16 : c * 16 + 16, :]] * 8, 0)
        for h in range(2):
            block = jnp.concatenate(
                [x[pl.ds(c * 4 + ri * 2 + h, 64, stride=32), :] for ri in range(2)], 0
            )
            both = dot3(split(block.T), pair(e))
            v, vs = both[:, :128], both[:, 128:]
            u = split(v * cos - vs * sin)
            us = split(vs * cos + v * sin)
            for kf in range(8):
                at = pl.ds((h * 8 + kf) * 128 + c * 16, 16)
                part = slice(kf * 16, kf * 16 + 16)
                uh[at, :] = u[0][part]
                ul[at, :] = u[1][part]
                sh[at, :] = us[0][part]
                sl[at, :] = us[1][part]
    ka = ka_ref[...]
    ka2 = ka * ka + FLOOR * FLOOR
    sign = jnp.where(lax.broadcasted_iota(jnp.int32, (128, 128), 1) < 64, -1.0, 1.0)

    def stack(first, second, col):
        parts = []
        for f in range(2):
            at = slice((col * 2 + f) * 128, (col * 2 + f + 1) * 128)
            parts.append(jnp.concatenate([first[at, :], second[at, :]], 0))
        return jnp.concatenate(parts, 1)

    for pr in range(4):
        q, qs = [], []
        for j in range(2):
            col = pr * 2 + j
            out = dot3(pair(w2), (stack(uh, sh, col), stack(ul, sl, col)))
            wb = kb[col]
            weight = LOCAL_WEIGHT + 1.0 / (ka2 + wb * wb)
            mixed = weight * (wb * out[:, :128] + ka * out[:, 128:])
            q.append(mixed)
            qs.append(pltpu.roll(mixed, 64, 1) * sign)
        rhs = jnp.concatenate([jnp.concatenate(q, 1), jnp.concatenate(qs, 1)], 0)
        back = dot3(pair(w3), split(rhs))
        for j in range(2):
            col = pr * 2 + j
            b = back[:128, j * 128 : (j + 1) * 128]
            bs = back[128:, j * 128 : (j + 1) * 128]
            y = split(b * tw[0] + bs * tw[1])
            for c in range(8):
                at = pl.ds(c * 128 + col * 16, 16)
                yh[at, :] = y[0][c * 16 : c * 16 + 16]
                yl[at, :] = y[1][c * 16 : c * 16 + 16]
    for c in range(8):
        rows = slice(c * 128, (c + 1) * 128)
        out = dot3(pair(e4), (yh[rows, :], yl[rows, :]), True)
        for ri in range(2):
            o[pl.ds(c * 2 + ri, 64, stride=16), :] = out[ri * 64 : (ri + 1) * 64]


def image_kernel(t, f4, m0i, tw, d4, o, vre, vim):
    for kg in range(4):
        block = [t[pl.ds(kg * 2 + ri, 128, stride=8), :].T for ri in range(2)]
        lhs = split(jnp.concatenate(block, 1))
        v = dot3(lhs, pair(f4))
        if kg == 0:
            special = dot3((lhs[0][:16], lhs[1][:16]), pair(m0i))
            v = jnp.concatenate([special, v[16:]], 0)
        for col in range(8):
            kk = kg * 8 + col
            re = v[col * 16 : col * 16 + 16, :128]
            im = v[col * 16 : col * 16 + 16, 128:]
            cos = tw[0, kk : kk + 1, :]
            sin = tw[1, kk : kk + 1, :]
            vre[kk * 16 : kk * 16 + 16, :] = re * cos - im * sin
            vim[kk * 16 : kk * 16 + 16, :] = im * cos + re * sin
    for grp in range(4):
        cols = []
        for j in range(4):
            at = pl.ds(grp * 4 + j, 32, stride=16)
            cols.append(jnp.concatenate([vre[at, :], vim[at, :]], 0))
        out = dot3(pair(d4), split(jnp.concatenate(cols, 1)))
        for j in range(4):
            i = grp * 4 + j
            for c in range(8):
                o[pl.ds(c * 128 + (i // 8) * 64 + i % 8, 8, stride=8), :] = out[
                    c * 8 : c * 8 + 8, j * 128 : (j + 1) * 128
                ]


def call(kernel, out_shape, scratch, *args, smem=(), **kw):
    specs = [
        pl.BlockSpec(memory_space=pltpu.SMEM if i in smem else pltpu.VMEM)
        for i in range(len(args))
    ]
    return pl.pallas_call(
        kernel,
        out_shape=jax.ShapeDtypeStruct(out_shape, F32),
        in_specs=specs,
        out_specs=pl.BlockSpec(memory_space=pltpu.VMEM),
        scratch_shapes=scratch,
        **kw,
    )(*args)


def two(table):
    return jnp.asarray(np.stack(table))


def pull(x, before, after, slopes, tile, rshift, pshift, frac):
    flip = lambda y: jnp.transpose(y, (0, 2, 1))
    return call(
        pull_kernel,
        (8, 8, 2, 16, 128),
        [pltpu.VMEM((2, 144, 1024), F32), pltpu.VMEM((128, 128), F32)],
        x, before, after, slopes, flip(tile), flip(rshift), flip(pshift), flip(frac),
    )


def column_transform(g):
    t = tables()
    return call(
        column_kernel,
        (2048, 128),
        [pltpu.VMEM((1024, 128), F32)] * 2,
        g, two(t["d1"]), jnp.asarray(t["tw1"]), two(t["f2"]), two(t["m0"]),
    )


def row_transform(x, device):
    t = tables()
    group, low = device // 4, device % 4
    kk = low * 8 + jnp.arange(8, dtype=jnp.int32)
    b = kk + 64 * group + jnp.where((kk == 0) & (group >= 64), 32, 0)
    kb = jnp.where(b > N // 2, b - N, b).astype(F32) * (2.0 * math.pi / N)
    return call(
        row_kernel,
        (1024, 128),
        [pltpu.VMEM((2048, 128), BF16)] * 4 + [pltpu.VMEM((1024, 128), BF16)] * 2,
        kb, x, two(t["e"]), jnp.asarray(t["tw2"]), two(t["w2"]), jnp.asarray(t["ka"]),
        two(t["w3"]), two(t["e4"]), smem=(0,),
    )


def image_transform(y):
    t = tables()
    return call(
        image_kernel,
        (1024, 128),
        [pltpu.VMEM((512, 128), F32)] * 2,
        y, two(t["f4"]), two(t["m0i"]), jnp.asarray(t["tw1"]), two(t["d4"]),
    )


def per_device(residual, field_slopes, source_tile, row_shift, pixel_shift, fraction):
    peers = lax.axis_size("rows")
    up = [(i, i + 1) for i in range(peers - 1)]
    down = [(j, i) for i, j in up]
    before = lax.ppermute(residual[:, -HALO:], "rows", up)
    after = lax.ppermute(residual[:, :HALO], "rows", down)
    flow = pull(
        residual, before, after, field_slopes, source_tile, row_shift, pixel_shift, fraction
    )
    flow = lax.all_to_all(flow, "cols", split_axis=0, concat_axis=0, tiled=True)
    spectra = column_transform(flow.reshape(2048, 128))
    spectra = lax.all_to_all(
        spectra.reshape(512, 4, 128), ("rows", "cols"), split_axis=0, concat_axis=0, tiled=True
    )
    device = lax.axis_index("rows") * lax.axis_size("cols") + lax.axis_index("cols")
    mixed = row_transform(spectra.reshape(2048, 128), device)
    mixed = lax.all_to_all(
        mixed.reshape(512, 2, 128), ("rows", "cols"), split_axis=0, concat_axis=0, tiled=True
    )
    image = image_transform(mixed.reshape(1024, 128))
    image = lax.all_to_all(
        image.reshape(8, 2, 8, 8, 128), "cols", split_axis=0, concat_axis=0, tiled=True
    )
    return jnp.transpose(image, (0, 1, 3, 2, 4)).reshape(128, 1024)


def solution(mesh):
    spec = P(None, "rows", "cols")
    return jax.shard_map(
        per_device,
        mesh=mesh,
        in_specs=(spec,) * 6,
        out_specs=P("rows", "cols"),
        check_vma=False,
    )
```

```python
import functools
import math

import jax
import jax.numpy as jnp
import ml_dtypes
import numpy as np
from jax import lax
from jax.experimental import pallas as pl
from jax.experimental.pallas import tpu as pltpu
from jax.sharding import PartitionSpec as P

N = 8192
TILE = 128
HALO = 8
SHIFT = 2
LOCAL_WEIGHT = 0.5
FLOOR = 8.0 * math.pi / N

F32 = jnp.float32
BF16 = jnp.bfloat16


def split_table(x):
    hi = x.astype(ml_dtypes.bfloat16)
    lo = (x - hi.astype(np.float64)).astype(ml_dtypes.bfloat16)
    return hi, lo


def cs(angle):
    return np.cos(angle), np.sin(angle)


@functools.lru_cache(maxsize=None)
def tables():
    two_pi = 2.0 * np.pi
    t = {}
    p = np.arange(64)[None, :]
    kk = np.arange(32)[:, None]
    c, s = cs(two_pi * ((p * kk) % 64) / 64)
    d1 = np.concatenate([c, -s], 0)
    d1[32] = (-1.0) ** np.arange(64)
    t["d1"] = split_table(d1)
    d4 = np.concatenate([2 * c, -2 * s], 0).T.copy()
    d4[:, 0] = 1.0
    d4[:, 32] = (-1.0) ** np.arange(64)
    t["d4"] = split_table(d4 / (N * N))
    q = np.arange(128)[None, :]
    c, s = cs(two_pi * (kk * q) / N)
    t["tw1"] = np.stack([c, s]).astype(np.float32)
    l = np.arange(128)[:, None]
    c, s = cs(two_pi * ((l * q) % 128) / 128)
    f2 = np.block([[c, s], [-s, c]])
    t["f2"] = split_table(f2)
    t["f4"] = split_table(np.block([[c, s], [-s, c]]))
    c32, s32 = cs(two_pi * ((q * (32 + 64 * l)) % N) / N)
    low = l < 64
    alt = np.broadcast_to((-1.0) ** q, (1, 128))
    m0 = np.zeros((256, 256))
    m0[:128, :128] = np.where(low, c, 0.0)
    m0[128:, :128] = np.where(low, -s, 0.0)
    m0[128:129, :128] = alt
    m0[:128, 128:] = np.where(low, 0.0, c32)
    m0[128:, 128:] = np.where(low, 0.0, -s32)
    t["m0"] = split_table(m0)
    mi = 2.0 * m0
    mi[0] *= 0.5
    mi[128] *= 0.5
    t["m0i"] = split_table(mi)
    r = np.arange(64)[:, None]
    m = np.arange(64)[None, :]
    c, s = cs(two_pi * ((r * m) % 64) / 64)
    e_re = np.concatenate([c, s], 0)
    e_im = np.concatenate([-s, c], 0)
    t["e"] = split_table(np.concatenate([e_re, e_im, -e_im, e_re], 1))
    t["e4"] = split_table(np.block([[c, -s], [s, c]]))
    q2 = np.arange(128)[:, None]
    mm = np.concatenate([np.arange(64), np.arange(64)])[None, :]
    c, s = cs(two_pi * (q2 * mm) / N)
    t["tw2"] = np.stack([c, s]).astype(np.float32)
    n = np.arange(128)[:, None]
    c, s = cs(two_pi * ((n * q2.T) % 128) / 128)
    t["w2"] = split_table(np.concatenate([c, -s], 1))
    t["w3"] = split_table(np.block([[s, -c], [c, s]]))
    a = mm + 64 * n
    signed = np.where(a > N // 2, a - N, np.where(a == N // 2, 0, a))
    t["ka"] = (signed * (two_pi / N)).astype(np.float32)
    return t


def split(x):
    hi = x.astype(BF16)
    return hi, (x - hi.astype(F32)).astype(BF16)


def dot(a, b, transposed=False):
    dims = (((1,), (1 if transposed else 0,)), ((), ()))
    return lax.dot_general(a, b, dims, preferred_element_type=F32)


def dot3(a, b, transposed=False):
    (ah, al), (bh, bl) = a, b
    return dot(ah, bh, transposed) + (dot(ah, bl, transposed) + dot(al, bh, transposed))


def pair(ref):
    return ref[0], ref[1]


def pull_kernel(x, before, after, slopes, tile, rshift, pshift, frac, o, padded, spots, wts, sc):
    padded[:, 0:HALO, :] = before[...].astype(F32)
    padded[:, HALO : HALO + 128, :] = x[...].astype(F32)
    padded[:, HALO + 128 :, :] = after[...].astype(F32)
    sc[:, :, 0:8, :] = jnp.zeros((2, 2, 8, 128), F32)
    sc[:, :, 136:144, :] = jnp.zeros((2, 2, 8, 128), F32)
    lane = lax.broadcasted_iota(jnp.int32, (8, 128), 1)

    def by_block(values):
        out = jnp.zeros((8, 128), values.dtype)
        for t in range(8):
            row = jnp.broadcast_to(values[t : t + 1, :], (8, 128))
            row = pltpu.roll(pltpu.roll(row, (16 * t + 16) % 128, 1), 0, 1, stride=16, stride_axis=0)
            out = jnp.where((lane >= 16 * t) & (lane < 16 * t + 16), row, out)
        return out

    for k in range(2):
        rows = slice(k * 8, k * 8 + 8)
        index = tile[k] * 32 + (lax.rem(lane, 16) + HALO) + rshift[k]
        spots[rows, :] = by_block(index)
        ps = by_block(pshift[k])
        f = by_block(frac[k])
        for oi in range(6):
            off = oi - SHIFT
            wts[oi, rows, :] = jnp.where(ps == off, 1.0 - f, 0.0) + jnp.where(
                ps + 1 == off, f, 0.0
            )
    place = lax.broadcasted_iota(jnp.int32, (256, 128), 0)

    def block(b, _):
        r0 = pl.multiple_of(b * 16, 16)
        window = [
            jnp.concatenate(
                [padded[p, pl.ds(r0, 32), u * 128 : (u + 1) * 128] for u in range(8)], 0
            )
            for p in range(2)
        ]
        window = jnp.concatenate(window, 1).astype(BF16)
        hot = jnp.concatenate(
            [
                jnp.where(place == spots[pl.ds(k * 8 + 7 - b, 1), :], 1.0, 0.0).astype(BF16)
                for k in range(2)
            ],
            1,
        )
        picked = lax.dot_general(
            window, hot, (((0,), (0,)), ((), ())), preferred_element_type=F32
        )
        for p in range(2):
            for k in range(2):
                sc[p, k, 8:136, :] = picked[p * 128 : p * 128 + 128, k * 128 : k * 128 + 128]
        got = []
        for p in range(2):
            total = None
            for oi in range(6):
                for k in range(2):
                    w = wts[oi, pl.ds(k * 8 + 7 - b, 1), :]
                    part = w * sc[p, k, 8 + oi - SHIFT : 136 + oi - SHIFT, :]
                    total = part if total is None else total + part
            got.append(total.T)
        for t in range(8):
            at = slice(t * 16, t * 16 + 16)
            first, second = got[0][at], got[1][at]
            s = [slopes[i, pl.ds(r0, 16), t * 128 : (t + 1) * 128].astype(F32) for i in range(4)]
            o[b, t, 0] = -(first * s[0] + second * s[1])
            o[b, t, 1] = -(first * s[2] + second * s[3])
        return 0

    lax.fori_loop(0, 8, block, 0)


def column_kernel(g, d1, tw, f2, m0, o, ure, uim):
    cos, sin = tw[0], tw[1]
    for grp in range(8):
        x = jnp.concatenate([g[pl.ds(grp * 4 + j, 64, stride=32), :] for j in range(4)], 1)
        v = dot3(pair(d1), split(x))
        for j in range(4):
            re = v[:32, j * 128 : (j + 1) * 128]
            im = v[32:, j * 128 : (j + 1) * 128]
            ure[pl.ds(grp * 4 + j, 32, stride=32), :] = re * cos + im * sin
            uim[pl.ds(grp * 4 + j, 32, stride=32), :] = im * cos - re * sin
    lane = lax.broadcasted_iota(jnp.int32, (256, 128), 1)
    for kg in range(4):
        rows = slice(kg * 256, (kg + 1) * 256)
        rhs = split(jnp.concatenate([ure[rows, :], uim[rows, :]], 1))
        out = dot3(pair(f2), rhs, True)
        for h in range(2):
            part = out[:, h * 128 : (h + 1) * 128]
            if kg == 0 and h == 0:
                special = dot3(pair(m0), (rhs[0][:128], rhs[1][:128]), True)
                part = jnp.where(lane < 32, special, part)
            for ri in range(2):
                o[pl.ds(kg * 4 + ri * 2 + h, 128, stride=16), :] = part[ri * 128 : (ri + 1) * 128]


def row_kernel(kb, x, e, tw, w2, ka_ref, w3, e4, o, uh, ul, sh, sl, yh, yl):
    for c in range(8):
        cos = jnp.concatenate([tw[0, c * 16 : c * 16 + 16, :]] * 8, 0)
        sin = jnp.concatenate([tw[1, c * 16 : c * 16 + 16, :]] * 8, 0)
        for h in range(2):
            block = jnp.concatenate(
                [x[pl.ds(c * 4 + ri * 2 + h, 64, stride=32), :] for ri in range(2)], 0
            )
            both = dot3(split(block.T), pair(e))
            v, vs = both[:, :128], both[:, 128:]
            u = split(v * cos - vs * sin)
            us = split(vs * cos + v * sin)
            for kf in range(8):
                at = pl.ds((h * 8 + kf) * 128 + c * 16, 16)
                part = slice(kf * 16, kf * 16 + 16)
                uh[at, :] = u[0][part]
                ul[at, :] = u[1][part]
                sh[at, :] = us[0][part]
                sl[at, :] = us[1][part]
    ka = ka_ref[...]
    ka2 = ka * ka + FLOOR * FLOOR
    sign = jnp.where(lax.broadcasted_iota(jnp.int32, (128, 128), 1) < 64, -1.0, 1.0)

    def stack(first, second, col):
        parts = []
        for f in range(2):
            at = slice((col * 2 + f) * 128, (col * 2 + f + 1) * 128)
            parts.append(jnp.concatenate([first[at, :], second[at, :]], 0))
        return jnp.concatenate(parts, 1)

    for pr in range(4):
        q, qs = [], []
        for j in range(2):
            col = pr * 2 + j
            out = dot3(pair(w2), (stack(uh, sh, col), stack(ul, sl, col)))
            wb = kb[col]
            weight = LOCAL_WEIGHT + 1.0 / (ka2 + wb * wb)
            mixed = weight * (wb * out[:, :128] + ka * out[:, 128:])
            q.append(mixed)
            qs.append(pltpu.roll(mixed, 64, 1) * sign)
        rhs = jnp.concatenate([jnp.concatenate(q, 1), jnp.concatenate(qs, 1)], 0)
        back = dot3(pair(w3), split(rhs))
        for j in range(2):
            col = pr * 2 + j
            b = back[:128, j * 128 : (j + 1) * 128]
            bs = back[128:, j * 128 : (j + 1) * 128]
            y = split(b * tw[0] + bs * tw[1])
            for c in range(8):
                at = pl.ds(c * 128 + col * 16, 16)
                yh[at, :] = y[0][c * 16 : c * 16 + 16]
                yl[at, :] = y[1][c * 16 : c * 16 + 16]
    for c in range(8):
        rows = slice(c * 128, (c + 1) * 128)
        out = dot3(pair(e4), (yh[rows, :], yl[rows, :]), True)
        for ri in range(2):
            o[pl.ds(c * 2 + ri, 64, stride=16), :] = out[ri * 64 : (ri + 1) * 64]


def image_kernel(t, f4, m0i, tw, d4, o, vre, vim):
    for kg in range(4):
        block = [t[pl.ds(kg * 2 + ri, 128, stride=8), :].T for ri in range(2)]
        lhs = split(jnp.concatenate(block, 1))
        v = dot3(lhs, pair(f4))
        if kg == 0:
            special = dot3((lhs[0][:16], lhs[1][:16]), pair(m0i))
            v = jnp.concatenate([special, v[16:]], 0)
        for col in range(8):
            kk = kg * 8 + col
            re = v[col * 16 : col * 16 + 16, :128]
            im = v[col * 16 : col * 16 + 16, 128:]
            cos = tw[0, kk : kk + 1, :]
            sin = tw[1, kk : kk + 1, :]
            vre[kk * 16 : kk * 16 + 16, :] = re * cos - im * sin
            vim[kk * 16 : kk * 16 + 16, :] = im * cos + re * sin
    for grp in range(4):
        cols = []
        for j in range(4):
            at = pl.ds(grp * 4 + j, 32, stride=16)
            cols.append(jnp.concatenate([vre[at, :], vim[at, :]], 0))
        out = dot3(pair(d4), split(jnp.concatenate(cols, 1)))
        for j in range(4):
            i = grp * 4 + j
            for c in range(8):
                o[pl.ds(c * 128 + (i // 8) * 64 + i % 8, 8, stride=8), :] = out[
                    c * 8 : c * 8 + 8, j * 128 : (j + 1) * 128
                ]


def call(kernel, out_shape, scratch, *args, smem=(), **kw):
    specs = [
        pl.BlockSpec(memory_space=pltpu.SMEM if i in smem else pltpu.VMEM)
        for i in range(len(args))
    ]
    return pl.pallas_call(
        kernel,
        out_shape=jax.ShapeDtypeStruct(out_shape, F32),
        in_specs=specs,
        out_specs=pl.BlockSpec(memory_space=pltpu.VMEM),
        scratch_shapes=scratch,
        **kw,
    )(*args)


def two(table):
    return jnp.asarray(np.stack(table))


def pull(x, before, after, slopes, tile, rshift, pshift, frac):
    flip = lambda y: jnp.transpose(y, (0, 2, 1))
    return call(
        pull_kernel,
        (8, 8, 2, 16, 128),
        [
            pltpu.VMEM((2, 144, 1024), F32),
            pltpu.VMEM((16, 128), jnp.int32),
            pltpu.VMEM((6, 16, 128), F32),
            pltpu.VMEM((2, 2, 144, 128), F32),
        ],
        x, before, after, slopes, flip(tile), flip(rshift), flip(pshift), flip(frac),
    )


def column_transform(g):
    t = tables()
    return call(
        column_kernel,
        (2048, 128),
        [pltpu.VMEM((1024, 128), F32)] * 2,
        g, two(t["d1"]), jnp.asarray(t["tw1"]), two(t["f2"]), two(t["m0"]),
    )


def row_transform(x, device):
    t = tables()
    group, low = device // 4, device % 4
    kk = low * 8 + jnp.arange(8, dtype=jnp.int32)
    b = kk + 64 * group + jnp.where((kk == 0) & (group >= 64), 32, 0)
    kb = jnp.where(b > N // 2, b - N, b).astype(F32) * (2.0 * math.pi / N)
    return call(
        row_kernel,
        (1024, 128),
        [pltpu.VMEM((2048, 128), BF16)] * 4 + [pltpu.VMEM((1024, 128), BF16)] * 2,
        kb, x, two(t["e"]), jnp.asarray(t["tw2"]), two(t["w2"]), jnp.asarray(t["ka"]),
        two(t["w3"]), two(t["e4"]), smem=(0,),
    )


def image_transform(y):
    t = tables()
    return call(
        image_kernel,
        (1024, 128),
        [pltpu.VMEM((512, 128), F32)] * 2,
        y, two(t["f4"]), two(t["m0i"]), jnp.asarray(t["tw1"]), two(t["d4"]),
    )


def per_device(residual, field_slopes, source_tile, row_shift, pixel_shift, fraction):
    peers = lax.axis_size("rows")
    up = [(i, i + 1) for i in range(peers - 1)]
    down = [(j, i) for i, j in up]
    before = lax.ppermute(residual[:, -HALO:], "rows", up)
    after = lax.ppermute(residual[:, :HALO], "rows", down)
    flow = pull(
        residual, before, after, field_slopes, source_tile, row_shift, pixel_shift, fraction
    )
    flow = lax.all_to_all(flow, "cols", split_axis=0, concat_axis=0, tiled=True)
    spectra = column_transform(flow.reshape(2048, 128))
    spectra = lax.all_to_all(
        spectra.reshape(512, 4, 128), ("rows", "cols"), split_axis=0, concat_axis=0, tiled=True
    )
    device = lax.axis_index("rows") * lax.axis_size("cols") + lax.axis_index("cols")
    mixed = row_transform(spectra.reshape(2048, 128), device)
    mixed = lax.all_to_all(
        mixed.reshape(512, 2, 128), ("rows", "cols"), split_axis=0, concat_axis=0, tiled=True
    )
    image = image_transform(mixed.reshape(1024, 128))
    image = lax.all_to_all(
        image.reshape(8, 2, 8, 8, 128), "cols", split_axis=0, concat_axis=0, tiled=True
    )
    return jnp.transpose(image, (0, 1, 3, 2, 4)).reshape(128, 1024)


def solution(mesh):
    spec = P(None, "rows", "cols")
    return jax.shard_map(
        per_device,
        mesh=mesh,
        in_specs=(spec,) * 6,
        out_specs=P("rows", "cols"),
        check_vma=False,
    )
```

```python
import functools
import math

import jax
import jax.numpy as jnp
import ml_dtypes
import numpy as np
from jax import lax
from jax.experimental import pallas as pl
from jax.experimental.pallas import tpu as pltpu
from jax.sharding import PartitionSpec as P

N = 8192
TILE = 128
HALO = 8
SHIFT = 2
LOCAL_WEIGHT = 0.5
FLOOR = 8.0 * math.pi / N

F32 = jnp.float32
BF16 = jnp.bfloat16
TINY = 1e-18
BIAS = 120.0
STEPS = 16380.0
CENTRE = 16384.0


def split_table(x):
    hi = x.astype(ml_dtypes.bfloat16)
    lo = (x - hi.astype(np.float64)).astype(ml_dtypes.bfloat16)
    return hi, lo


def cs(angle):
    return np.cos(angle), np.sin(angle)


@functools.lru_cache(maxsize=None)
def tables():
    two_pi = 2.0 * np.pi
    t = {}
    p = np.arange(64)[None, :]
    kk = np.arange(32)[:, None]
    c, s = cs(two_pi * ((p * kk) % 64) / 64)
    d1 = np.concatenate([c, -s], 0)
    d1[32] = (-1.0) ** np.arange(64)
    t["d1"] = split_table(d1)
    d4 = np.concatenate([2 * c, -2 * s], 0).T.copy()
    d4[:, 0] = 1.0
    d4[:, 32] = (-1.0) ** np.arange(64)
    t["d4"] = split_table(d4 / (N * N))
    q = np.arange(128)[None, :]
    c, s = cs(two_pi * (kk * q) / N)
    t["tw1"] = np.stack([c, s]).astype(np.float32)
    l = np.arange(128)[:, None]
    c, s = cs(two_pi * ((l * q) % 128) / 128)
    f2 = np.block([[c, s], [-s, c]])
    t["f2"] = split_table(f2)
    t["f4"] = split_table(np.block([[c, s], [-s, c]]))
    c32, s32 = cs(two_pi * ((q * (32 + 64 * l)) % N) / N)
    low = l < 64
    alt = np.broadcast_to((-1.0) ** q, (1, 128))
    m0 = np.zeros((256, 256))
    m0[:128, :128] = np.where(low, c, 0.0)
    m0[128:, :128] = np.where(low, -s, 0.0)
    m0[128:129, :128] = alt
    m0[:128, 128:] = np.where(low, 0.0, c32)
    m0[128:, 128:] = np.where(low, 0.0, -s32)
    t["m0"] = split_table(m0)
    mi = 2.0 * m0
    mi[0] *= 0.5
    mi[128] *= 0.5
    t["m0i"] = split_table(mi)
    r = np.arange(64)[:, None]
    m = np.arange(64)[None, :]
    c, s = cs(two_pi * ((r * m) % 64) / 64)
    e_re = np.concatenate([c, s], 0)
    e_im = np.concatenate([-s, c], 0)
    t["e"] = split_table(np.concatenate([e_re, e_im, -e_im, e_re], 1))
    t["e4"] = split_table(np.block([[c, -s], [s, c]]))
    q2 = np.arange(128)[:, None]
    mm = np.concatenate([np.arange(64), np.arange(64)])[None, :]
    c, s = cs(two_pi * (q2 * mm) / N)
    t["tw2"] = np.stack([c, s]).astype(np.float32)
    n = np.arange(128)[:, None]
    c, s = cs(two_pi * ((n * q2.T) % 128) / 128)
    t["w2"] = split_table(np.concatenate([c, -s], 1))
    t["w3"] = split_table(np.block([[s, -c], [c, s]]))
    a = mm + 64 * n
    signed = np.where(a > N // 2, a - N, np.where(a == N // 2, 0, a))
    t["ka"] = (signed * (two_pi / N)).astype(np.float32)
    return t


def split(x):
    hi = x.astype(BF16)
    return hi, (x - hi.astype(F32)).astype(BF16)


def dot(a, b, transposed=False):
    dims = (((1,), (1 if transposed else 0,)), ((), ()))
    return lax.dot_general(a, b, dims, preferred_element_type=F32)


def dot3(a, b, transposed=False):
    (ah, al), (bh, bl) = a, b
    return dot(ah, bh, transposed) + (dot(ah, bl, transposed) + dot(al, bh, transposed))


def pair(ref):
    return ref[0], ref[1]


def spread(x, join):
    x = join(x, pltpu.roll(x, 64, 1))
    return join(x, pltpu.roll(x, 32, 1))


def lane_field(shape):
    return lax.shift_left(
        lax.shift_right_logical(lax.broadcasted_iota(jnp.int32, shape, 1), 5), 1
    )


def encode(x, y):
    peak = spread(jnp.maximum(jnp.abs(x), jnp.abs(y)), jnp.maximum)
    level = jnp.ceil(2.0 * jnp.log2(jnp.maximum(peak, TINY))) + BIAS
    level = jnp.clip(level, 0.0, 255.0)
    gain = jnp.exp2((BIAS - level) * 0.5) * STEPS
    code = level.astype(jnp.int32)
    bits = lax.shift_right_logical(code, lane_field(x.shape)) & 3
    qx = (x * gain + (CENTRE + 0.5)).astype(jnp.int32)
    qy = (y * gain + (CENTRE + 0.5)).astype(jnp.int32)
    return qx | lax.shift_left(qy, 15) | lax.shift_left(bits, 30)


def decode(word):
    bits = lax.shift_right_logical(word, 30) & 3
    code = spread(lax.shift_left(bits, lane_field(word.shape)), jnp.add)
    scale = jnp.exp2((code.astype(F32) - BIAS) * 0.5) * (1.0 / STEPS)
    x = (word & 32767).astype(F32) - CENTRE
    y = (lax.shift_right_logical(word, 15) & 32767).astype(F32) - CENTRE
    return x * scale, y * scale


def pull_kernel(x, before, after, slopes, tile, rshift, pshift, frac, o, padded, spots, wts, sc):
    padded[:, 0:HALO, :] = before[...].astype(F32)
    padded[:, HALO : HALO + 128, :] = x[...].astype(F32)
    padded[:, HALO + 128 :, :] = after[...].astype(F32)
    sc[:, :, 0:8, :] = jnp.zeros((2, 2, 8, 128), F32)
    sc[:, :, 136:144, :] = jnp.zeros((2, 2, 8, 128), F32)
    lane = lax.broadcasted_iota(jnp.int32, (8, 128), 1)

    def by_block(values):
        out = jnp.zeros((8, 128), values.dtype)
        for t in range(8):
            row = jnp.broadcast_to(values[t : t + 1, :], (8, 128))
            row = pltpu.roll(pltpu.roll(row, (16 * t + 16) % 128, 1), 0, 1, stride=16, stride_axis=0)
            out = jnp.where((lane >= 16 * t) & (lane < 16 * t + 16), row, out)
        return out

    for k in range(2):
        rows = slice(k * 8, k * 8 + 8)
        index = tile[k] * 32 + (lax.rem(lane, 16) + HALO) + rshift[k]
        spots[rows, :] = by_block(index)
        ps = by_block(pshift[k])
        f = by_block(frac[k])
        for oi in range(6):
            off = oi - SHIFT
            wts[oi, rows, :] = jnp.where(ps == off, 1.0 - f, 0.0) + jnp.where(
                ps + 1 == off, f, 0.0
            )
    place = lax.broadcasted_iota(jnp.int32, (256, 128), 0)

    def block(b, _):
        r0 = pl.multiple_of(b * 16, 16)
        window = [
            jnp.concatenate(
                [padded[p, pl.ds(r0, 32), u * 128 : (u + 1) * 128] for u in range(8)], 0
            )
            for p in range(2)
        ]
        window = jnp.concatenate(window, 1).astype(BF16)
        hot = jnp.concatenate(
            [
                jnp.where(place == spots[pl.ds(k * 8 + 7 - b, 1), :], 1.0, 0.0).astype(BF16)
                for k in range(2)
            ],
            1,
        )
        picked = lax.dot_general(
            window, hot, (((0,), (0,)), ((), ())), preferred_element_type=F32
        )
        for p in range(2):
            for k in range(2):
                sc[p, k, 8:136, :] = picked[p * 128 : p * 128 + 128, k * 128 : k * 128 + 128]
        got = []
        for p in range(2):
            total = None
            for oi in range(6):
                for k in range(2):
                    w = wts[oi, pl.ds(k * 8 + 7 - b, 1), :]
                    part = w * sc[p, k, 8 + oi - SHIFT : 136 + oi - SHIFT, :]
                    total = part if total is None else total + part
            got.append(total.T)
        for t in range(8):
            at = slice(t * 16, t * 16 + 16)
            first, second = got[0][at], got[1][at]
            s = [slopes[i, pl.ds(r0, 16), t * 128 : (t + 1) * 128].astype(F32) for i in range(4)]
            o[b, t, 0] = -(first * s[0] + second * s[1])
            o[b, t, 1] = -(first * s[2] + second * s[3])
        return 0

    lax.fori_loop(0, 8, block, 0)


def column_kernel(g, d1, tw, f2, m0, o, ure, uim):
    cos, sin = tw[0], tw[1]
    for grp in range(8):
        x = jnp.concatenate([g[pl.ds(grp * 4 + j, 64, stride=32), :] for j in range(4)], 1)
        v = dot3(pair(d1), split(x))
        for j in range(4):
            re = v[:32, j * 128 : (j + 1) * 128]
            im = v[32:, j * 128 : (j + 1) * 128]
            ure[pl.ds(grp * 4 + j, 32, stride=32), :] = re * cos + im * sin
            uim[pl.ds(grp * 4 + j, 32, stride=32), :] = im * cos - re * sin
    lane = lax.broadcasted_iota(jnp.int32, (256, 128), 1)
    for kg in range(4):
        rows = slice(kg * 256, (kg + 1) * 256)
        rhs = split(jnp.concatenate([ure[rows, :], uim[rows, :]], 1))
        out = dot3(pair(f2), rhs, True)
        for h in range(2):
            part = out[:, h * 128 : (h + 1) * 128]
            if kg == 0 and h == 0:
                special = dot3(pair(m0), (rhs[0][:128], rhs[1][:128]), True)
                part = jnp.where(lane < 32, special, part)
            o[pl.ds(kg * 2 + h, 128, stride=8), :] = encode(part[:128], part[128:])


def row_kernel(kb, x, e, tw, w2, ka_ref, w3, e4, o, uh, ul, sh, sl, yh, yl):
    for c in range(8):
        cos = jnp.concatenate([tw[0, c * 16 : c * 16 + 16, :]] * 8, 0)
        sin = jnp.concatenate([tw[1, c * 16 : c * 16 + 16, :]] * 8, 0)
        for h in range(2):
            block = jnp.concatenate(decode(x[pl.ds(c * 2 + h, 64, stride=16), :]), 0)
            both = dot3(split(block.T), pair(e))
            v, vs = both[:, :128], both[:, 128:]
            u = split(v * cos - vs * sin)
            us = split(vs * cos + v * sin)
            for kf in range(8):
                at = pl.ds((h * 8 + kf) * 128 + c * 16, 16)
                part = slice(kf * 16, kf * 16 + 16)
                uh[at, :] = u[0][part]
                ul[at, :] = u[1][part]
                sh[at, :] = us[0][part]
                sl[at, :] = us[1][part]
    ka = ka_ref[...]
    ka2 = ka * ka + FLOOR * FLOOR
    sign = jnp.where(lax.broadcasted_iota(jnp.int32, (128, 128), 1) < 64, -1.0, 1.0)

    def stack(first, second, col):
        parts = []
        for f in range(2):
            at = slice((col * 2 + f) * 128, (col * 2 + f + 1) * 128)
            parts.append(jnp.concatenate([first[at, :], second[at, :]], 0))
        return jnp.concatenate(parts, 1)

    for pr in range(4):
        q, qs = [], []
        for j in range(2):
            col = pr * 2 + j
            out = dot3(pair(w2), (stack(uh, sh, col), stack(ul, sl, col)))
            wb = kb[col]
            weight = LOCAL_WEIGHT + 1.0 / (ka2 + wb * wb)
            mixed = weight * (wb * out[:, :128] + ka * out[:, 128:])
            q.append(mixed)
            qs.append(pltpu.roll(mixed, 64, 1) * sign)
        rhs = jnp.concatenate([jnp.concatenate(q, 1), jnp.concatenate(qs, 1)], 0)
        back = dot3(pair(w3), split(rhs))
        for j in range(2):
            col = pr * 2 + j
            b = back[:128, j * 128 : (j + 1) * 128]
            bs = back[128:, j * 128 : (j + 1) * 128]
            y = split(b * tw[0] + bs * tw[1])
            for c in range(8):
                at = pl.ds(c * 128 + col * 16, 16)
                yh[at, :] = y[0][c * 16 : c * 16 + 16]
                yl[at, :] = y[1][c * 16 : c * 16 + 16]
    for c in range(8):
        rows = slice(c * 128, (c + 1) * 128)
        out = dot3(pair(e4), (yh[rows, :], yl[rows, :]), True)
        o[pl.ds(c, 64, stride=8), :] = encode(out[:64], out[64:])


def image_kernel(t, f4, m0i, tw, d4, o, vre, vim):
    for kg in range(4):
        block = decode(t[pl.ds(kg, 128, stride=4), :])
        lhs = split(jnp.concatenate([part.T for part in block], 1))
        v = dot3(lhs, pair(f4))
        if kg == 0:
            special = dot3((lhs[0][:16], lhs[1][:16]), pair(m0i))
            v = jnp.concatenate([special, v[16:]], 0)
        for col in range(8):
            kk = kg * 8 + col
            re = v[col * 16 : col * 16 + 16, :128]
            im = v[col * 16 : col * 16 + 16, 128:]
            cos = tw[0, kk : kk + 1, :]
            sin = tw[1, kk : kk + 1, :]
            vre[kk * 16 : kk * 16 + 16, :] = re * cos - im * sin
            vim[kk * 16 : kk * 16 + 16, :] = im * cos + re * sin
    for grp in range(4):
        cols = []
        for j in range(4):
            at = pl.ds(grp * 4 + j, 32, stride=16)
            cols.append(jnp.concatenate([vre[at, :], vim[at, :]], 0))
        out = dot3(pair(d4), split(jnp.concatenate(cols, 1)))
        for j in range(4):
            i = grp * 4 + j
            for c in range(8):
                o[pl.ds(c * 128 + (i // 8) * 64 + i % 8, 8, stride=8), :] = out[
                    c * 8 : c * 8 + 8, j * 128 : (j + 1) * 128
                ]


def call(kernel, out_shape, scratch, *args, smem=(), dtype=F32, **kw):
    specs = [
        pl.BlockSpec(memory_space=pltpu.SMEM if i in smem else pltpu.VMEM)
        for i in range(len(args))
    ]
    return pl.pallas_call(
        kernel,
        out_shape=jax.ShapeDtypeStruct(out_shape, dtype),
        in_specs=specs,
        out_specs=pl.BlockSpec(memory_space=pltpu.VMEM),
        scratch_shapes=scratch,
        **kw,
    )(*args)


def two(table):
    return jnp.asarray(np.stack(table))


def pull(x, before, after, slopes, tile, rshift, pshift, frac):
    flip = lambda y: jnp.transpose(y, (0, 2, 1))
    return call(
        pull_kernel,
        (8, 8, 2, 16, 128),
        [
            pltpu.VMEM((2, 144, 1024), F32),
            pltpu.VMEM((16, 128), jnp.int32),
            pltpu.VMEM((6, 16, 128), F32),
            pltpu.VMEM((2, 2, 144, 128), F32),
        ],
        x, before, after, slopes, flip(tile), flip(rshift), flip(pshift), flip(frac),
    )


def column_transform(g):
    t = tables()
    return call(
        column_kernel,
        (1024, 128),
        [pltpu.VMEM((1024, 128), F32)] * 2,
        g, two(t["d1"]), jnp.asarray(t["tw1"]), two(t["f2"]), two(t["m0"]),
        dtype=jnp.int32,
    )


def row_transform(x, device):
    t = tables()
    group, low = device // 4, device % 4
    kk = low * 8 + jnp.arange(8, dtype=jnp.int32)
    b = kk + 64 * group + jnp.where((kk == 0) & (group >= 64), 32, 0)
    kb = jnp.where(b > N // 2, b - N, b).astype(F32) * (2.0 * math.pi / N)
    return call(
        row_kernel,
        (512, 128),
        [pltpu.VMEM((2048, 128), BF16)] * 4 + [pltpu.VMEM((1024, 128), BF16)] * 2,
        kb, x, two(t["e"]), jnp.asarray(t["tw2"]), two(t["w2"]), jnp.asarray(t["ka"]),
        two(t["w3"]), two(t["e4"]), smem=(0,), dtype=jnp.int32,
    )


def image_transform(y):
    t = tables()
    return call(
        image_kernel,
        (1024, 128),
        [pltpu.VMEM((512, 128), F32)] * 2,
        y, two(t["f4"]), two(t["m0i"]), jnp.asarray(t["tw1"]), two(t["d4"]),
    )


def per_device(residual, field_slopes, source_tile, row_shift, pixel_shift, fraction):
    peers = lax.axis_size("rows")
    up = [(i, i + 1) for i in range(peers - 1)]
    down = [(j, i) for i, j in up]
    before = lax.ppermute(residual[:, -HALO:], "rows", up)
    after = lax.ppermute(residual[:, :HALO], "rows", down)
    flow = pull(
        residual, before, after, field_slopes, source_tile, row_shift, pixel_shift, fraction
    )
    flow = lax.all_to_all(flow, "cols", split_axis=0, concat_axis=0, tiled=True)
    spectra = column_transform(flow.reshape(2048, 128))
    spectra = lax.all_to_all(
        spectra.reshape(512, 2, 128), ("rows", "cols"), split_axis=0, concat_axis=0, tiled=True
    )
    device = lax.axis_index("rows") * lax.axis_size("cols") + lax.axis_index("cols")
    mixed = row_transform(spectra.reshape(1024, 128), device)
    mixed = lax.all_to_all(
        mixed.reshape(512, 1, 128), ("rows", "cols"), split_axis=0, concat_axis=0, tiled=True
    )
    image = image_transform(mixed.reshape(512, 128))
    image = lax.all_to_all(
        image.reshape(8, 2, 8, 8, 128), "cols", split_axis=0, concat_axis=0, tiled=True
    )
    return jnp.transpose(image, (0, 1, 3, 2, 4)).reshape(128, 1024)


def solution(mesh):
    spec = P(None, "rows", "cols")
    return jax.shard_map(
        per_device,
        mesh=mesh,
        in_specs=(spec,) * 6,
        out_specs=P("rows", "cols"),
        check_vma=False,
    )
```

```python
import functools
import math

import jax
import jax.numpy as jnp
import ml_dtypes
import numpy as np
from jax import lax
from jax.experimental import pallas as pl
from jax.experimental.pallas import tpu as pltpu
from jax.sharding import PartitionSpec as P

N = 8192
TILE = 128
HALO = 8
SHIFT = 2
LOCAL_WEIGHT = 0.5
FLOOR = 8.0 * math.pi / N

F32 = jnp.float32
BF16 = jnp.bfloat16
TINY = 1e-18
BIAS = 120.0
STEPS = 16380.0
CENTRE = 16384.0


def split_table(x):
    hi = x.astype(ml_dtypes.bfloat16)
    lo = (x - hi.astype(np.float64)).astype(ml_dtypes.bfloat16)
    return hi, lo


def cs(angle):
    return np.cos(angle), np.sin(angle)


@functools.lru_cache(maxsize=None)
def tables():
    two_pi = 2.0 * np.pi
    t = {}
    p = np.arange(64)[None, :]
    kk = np.arange(32)[:, None]
    c, s = cs(two_pi * ((p * kk) % 64) / 64)
    d1 = np.concatenate([c, -s], 0)
    d1[32] = (-1.0) ** np.arange(64)
    t["d1"] = split_table(d1)
    d4 = np.concatenate([2 * c, -2 * s], 0).T.copy()
    d4[:, 0] = 1.0
    d4[:, 32] = (-1.0) ** np.arange(64)
    t["d4"] = split_table(d4 / (N * N))
    q = np.arange(128)[None, :]
    c, s = cs(two_pi * (kk * q) / N)
    t["tw1"] = np.stack([c, s]).astype(np.float32)
    l = np.arange(128)[:, None]
    c, s = cs(two_pi * ((l * q) % 128) / 128)
    f2 = np.block([[c, s], [-s, c]])
    order = np.concatenate([np.arange(0, 128, 2), np.arange(1, 128, 2)])
    order = np.concatenate([order, 128 + order])
    t["f2"] = split_table(f2[order])
    t["f4"] = split_table(np.block([[c, s], [-s, c]]))
    c32, s32 = cs(two_pi * ((q * (32 + 64 * l)) % N) / N)
    low = l < 64
    alt = np.broadcast_to((-1.0) ** q, (1, 128))
    m0 = np.zeros((256, 256))
    m0[:128, :128] = np.where(low, c, 0.0)
    m0[128:, :128] = np.where(low, -s, 0.0)
    m0[128:129, :128] = alt
    m0[:128, 128:] = np.where(low, 0.0, c32)
    m0[128:, 128:] = np.where(low, 0.0, -s32)
    t["m0"] = split_table(m0[order])
    mi = 2.0 * m0
    mi[0] *= 0.5
    mi[128] *= 0.5
    t["m0i"] = split_table(mi)
    r = np.arange(64)[:, None]
    m = np.arange(64)[None, :]
    c, s = cs(two_pi * ((r * m) % 64) / 64)
    e_re = np.concatenate([c, s], 0)
    e_im = np.concatenate([-s, c], 0)
    t["e"] = split_table(np.concatenate([e_re, e_im, -e_im, e_re], 1))
    t["e4"] = split_table(np.block([[c, -s], [s, c]]))
    q2 = np.arange(128)[:, None]
    mm = np.concatenate([np.arange(64), np.arange(64)])[None, :]
    c, s = cs(two_pi * (q2 * mm) / N)
    t["tw2"] = np.stack([c, s]).astype(np.float32)
    n = np.arange(128)[:, None]
    c, s = cs(two_pi * ((n * q2.T) % 128) / 128)
    t["w2"] = split_table(np.concatenate([c, -s], 1))
    t["w3"] = split_table(np.block([[s, -c], [c, s]]))
    a = mm + 64 * n
    signed = np.where(a > N // 2, a - N, np.where(a == N // 2, 0, a))
    t["ka"] = (signed * (two_pi / N)).astype(np.float32)
    return t


def split(x):
    hi = x.astype(BF16)
    return hi, (x - hi.astype(F32)).astype(BF16)


def dot(a, b, transposed=False):
    dims = (((1,), (1 if transposed else 0,)), ((), ()))
    return lax.dot_general(a, b, dims, preferred_element_type=F32)


def dot3(a, b, transposed=False):
    (ah, al), (bh, bl) = a, b
    return dot(ah, bh, transposed) + (dot(ah, bl, transposed) + dot(al, bh, transposed))


def pair(ref):
    return ref[0], ref[1]


MESH = pl.DeviceIdType.MESH
ROWS, COLS = 64, 8


def here():
    return lax.axis_index("rows"), lax.axis_index("cols")


def greet(rows):
    r, c = here()
    barrier = pltpu.get_barrier_semaphore()
    for i in range(1, COLS):
        peer = (r, lax.rem(c + i, COLS))
        pl.semaphore_signal(barrier, inc=1, device_id=peer, device_id_type=MESH)
    if rows:

        def signal(i, _):
            peer = (lax.rem(r + i, ROWS), c)
            pl.semaphore_signal(barrier, inc=1, device_id=peer, device_id_type=MESH)
            return 0

        lax.fori_loop(1, ROWS, signal, 0)


def gather(rows):
    count = COLS - 1 + (ROWS - 1 if rows else 0)
    pl.semaphore_wait(pltpu.get_barrier_semaphore(), count)


def to_col(peer, src, dst, sems):
    r, c = here()

    @pl.when(peer != c)
    def _():
        pltpu.make_async_remote_copy(
            src_ref=src.at[peer],
            dst_ref=dst.at[c],
            send_sem=sems[0],
            recv_sem=sems[1],
            device_id=(r, peer),
            device_id_type=MESH,
        ).start()


def finish(ref, count, sem):
    part = ref.at[pl.ds(0, count)]
    pltpu.make_async_copy(part, part, sem).wait()


def to_rows(src, dst, sems):
    r, c = here()

    def send(i, _):
        peer = lax.rem(r + i, ROWS)
        pltpu.make_async_remote_copy(
            src_ref=src.at[:, peer],
            dst_ref=dst.at[r],
            send_sem=sems[0],
            recv_sem=sems[1],
            device_id=(peer, c),
            device_id_type=MESH,
        ).start()
        return 0

    lax.fori_loop(1, ROWS, send, 0)
    dst[r] = src[:, r]
    finish(dst, ROWS - 1, sems[1])


def spread(x, join):
    x = join(x, pltpu.roll(x, 64, 1))
    return join(x, pltpu.roll(x, 32, 1))


def lane_field(shape):
    return lax.shift_left(
        lax.shift_right_logical(lax.broadcasted_iota(jnp.int32, shape, 1), 5), 1
    )


def encode(x, y):
    peak = spread(jnp.maximum(jnp.abs(x), jnp.abs(y)), jnp.maximum)
    level = jnp.ceil(2.0 * jnp.log2(jnp.maximum(peak, TINY))) + BIAS
    level = jnp.clip(level, 0.0, 255.0)
    gain = jnp.exp2((BIAS - level) * 0.5) * STEPS
    code = level.astype(jnp.int32)
    bits = lax.shift_right_logical(code, lane_field(x.shape)) & 3
    qx = (x * gain + (CENTRE + 0.5)).astype(jnp.int32)
    qy = (y * gain + (CENTRE + 0.5)).astype(jnp.int32)
    return qx | lax.shift_left(qy, 15) | lax.shift_left(bits, 30)


def decode(word):
    bits = lax.shift_right_logical(word, 30) & 3
    code = spread(lax.shift_left(bits, lane_field(word.shape)), jnp.add)
    scale = jnp.exp2((code.astype(F32) - BIAS) * 0.5) * (1.0 / STEPS)
    x = (word & 32767).astype(F32) - CENTRE
    y = (lax.shift_right_logical(word, 15) & 32767).astype(F32) - CENTRE
    return x * scale, y * scale


def pull_kernel(net, x, before, after, slopes, tile, rshift, pshift, frac, o, s1, padded, spots, wts, sc, *sems):
    own = here()[1] if net else 0
    if net:
        greet(False)
    padded[:, 0:HALO, :] = before[...].astype(F32)
    padded[:, HALO : HALO + 128, :] = x[...].astype(F32)
    padded[:, HALO + 128 :, :] = after[...].astype(F32)
    sc[:, :, 0:8, :] = jnp.zeros((2, 2, 8, 128), F32)
    sc[:, :, 136:144, :] = jnp.zeros((2, 2, 8, 128), F32)
    lane = lax.broadcasted_iota(jnp.int32, (8, 128), 1)

    def by_block(values):
        out = jnp.zeros((8, 128), values.dtype)
        for t in range(8):
            row = jnp.broadcast_to(values[t : t + 1, :], (8, 128))
            row = pltpu.roll(pltpu.roll(row, (16 * t + 16) % 128, 1), 0, 1, stride=16, stride_axis=0)
            out = jnp.where((lane >= 16 * t) & (lane < 16 * t + 16), row, out)
        return out

    for k in range(2):
        rows = slice(k * 8, k * 8 + 8)
        index = tile[k] * 32 + (lax.rem(lane, 16) + HALO) + rshift[k]
        spots[rows, :] = by_block(index)
        ps = by_block(pshift[k])
        f = by_block(frac[k])
        for oi in range(6):
            off = oi - SHIFT
            wts[oi, rows, :] = jnp.where(ps == off, 1.0 - f, 0.0) + jnp.where(
                ps + 1 == off, f, 0.0
            )
    place = lax.broadcasted_iota(jnp.int32, (256, 128), 0)

    def block(n, _):
        b = lax.rem(own + 1 + n, COLS)
        r0 = pl.multiple_of(b * 16, 16)
        window = [
            jnp.concatenate(
                [padded[p, pl.ds(r0, 32), u * 128 : (u + 1) * 128] for u in range(8)], 0
            )
            for p in range(2)
        ]
        window = jnp.concatenate(window, 1).astype(BF16)
        hot = jnp.concatenate(
            [
                jnp.where(place == spots[pl.ds(k * 8 + 7 - b, 1), :], 1.0, 0.0).astype(BF16)
                for k in range(2)
            ],
            1,
        )
        picked = lax.dot_general(
            window, hot, (((0,), (0,)), ((), ())), preferred_element_type=F32
        )
        for p in range(2):
            for k in range(2):
                sc[p, k, 8:136, :] = picked[p * 128 : p * 128 + 128, k * 128 : k * 128 + 128]
        got = []
        for p in range(2):
            total = None
            for oi in range(6):
                for k in range(2):
                    w = wts[oi, pl.ds(k * 8 + 7 - b, 1), :]
                    part = w * sc[p, k, 8 + oi - SHIFT : 136 + oi - SHIFT, :]
                    total = part if total is None else total + part
            got.append(total.T)
        for t in range(8):
            at = slice(t * 16, t * 16 + 16)
            first, second = got[0][at], got[1][at]
            s = [slopes[i, pl.ds(r0, 16), t * 128 : (t + 1) * 128].astype(F32) for i in range(4)]
            across = -(first * s[0] + second * s[1])
            down = -(first * s[2] + second * s[3])
            s1[b, t * 16 : t * 16 + 16, :] = encode(across, down)
        if net:

            @pl.when(n == 1)
            def _():
                gather(False)

            @pl.when(n > 0)
            def _():
                to_col(lax.rem(own + n, COLS), s1, o, sems)

        return 0

    lax.fori_loop(0, 8, block, 0)
    if net:
        o[own] = s1[own]
        finish(o, COLS - 1, sems[1])
        finish(s1, COLS - 1, sems[0])
    else:
        o[...] = s1[...]


def column_kernel(net, g, d1, tw, f2, m0, o, s1, r1, ure, uim, *sems):
    if net:
        greet(True)
    flat = s1.reshape(1024, 128) if net else s1
    cos, sin = tw[0], tw[1]
    for grp in range(8):
        x, at = [], []
        for i in (2 * grp, 2 * grp + 1):
            x += decode(g[pl.ds(i, 64, stride=16), :])
            at += [i, 16 + i]
        v = dot3(pair(d1), split(jnp.concatenate(x, 1)))
        for j in range(4):
            re = v[:32, j * 128 : (j + 1) * 128]
            im = v[32:, j * 128 : (j + 1) * 128]
            ure[pl.ds(at[j], 32, stride=32), :] = re * cos + im * sin
            uim[pl.ds(at[j], 32, stride=32), :] = im * cos - re * sin
    lane = lax.broadcasted_iota(jnp.int32, (256, 128), 1)

    def send(kg):
        if net and kg >= 0:
            if kg == 0:
                gather(True)
            to_col(kg, s1, r1, sems[:2])
            to_col(kg + 4, s1, r1, sems[:2])

    for kg in range(4):
        rows = slice(kg * 256, (kg + 1) * 256)
        rhs = split(jnp.concatenate([ure[rows, :], uim[rows, :]], 1))
        out = dot3(pair(f2), rhs, True)
        for h in range(2):
            part = out[:, h * 128 : (h + 1) * 128]
            if kg == 0 and h == 0:
                special = dot3(pair(m0), (rhs[0][:128], rhs[1][:128]), True)
                part = jnp.where(lane < 32, special, part)
            word = encode(part[:128], part[128:])
            for half in range(2):
                at = pl.ds((half * 4 + kg) * 128 + h, 64, stride=2)
                flat[at, :] = word[half * 64 : half * 64 + 64]
        send(kg - 1)
    send(3)
    if net:
        own = here()[1]
        r1[own] = s1[own]
        finish(r1, COLS - 1, sems[1])
        to_rows(r1, o, sems[2:])
        finish(s1, COLS - 1, sems[0])
        finish(o, ROWS - 1, sems[2])
    else:
        o[...] = s1[...]


def row_kernel(net, kb, x, e, tw, w2, ka_ref, w3, e4, o, s1, r1, uh, ul, sh, sl, yh, yl, *sems):
    if net:
        greet(True)
    flat = s1.reshape(512, 128) if net else s1
    for c in range(8):
        cos = jnp.concatenate([tw[0, c * 16 : c * 16 + 16, :]] * 8, 0)
        sin = jnp.concatenate([tw[1, c * 16 : c * 16 + 16, :]] * 8, 0)
        for h in range(2):
            block = jnp.concatenate(decode(x[pl.ds(c * 2 + h, 64, stride=16), :]), 0)
            both = dot3(split(block.T), pair(e))
            v, vs = both[:, :128], both[:, 128:]
            u = split(v * cos - vs * sin)
            us = split(vs * cos + v * sin)
            for kf in range(8):
                at = pl.ds((h * 8 + kf) * 128 + c * 16, 16)
                part = slice(kf * 16, kf * 16 + 16)
                uh[at, :] = u[0][part]
                ul[at, :] = u[1][part]
                sh[at, :] = us[0][part]
                sl[at, :] = us[1][part]
    ka = ka_ref[...]
    ka2 = ka * ka + FLOOR * FLOOR
    sign = jnp.where(lax.broadcasted_iota(jnp.int32, (128, 128), 1) < 64, -1.0, 1.0)

    def stack(first, second, col):
        parts = []
        for f in range(2):
            at = slice((col * 2 + f) * 128, (col * 2 + f + 1) * 128)
            parts.append(jnp.concatenate([first[at, :], second[at, :]], 0))
        return jnp.concatenate(parts, 1)

    for pr in range(4):
        q, qs = [], []
        for j in range(2):
            col = pr * 2 + j
            out = dot3(pair(w2), (stack(uh, sh, col), stack(ul, sl, col)))
            wb = kb[col]
            weight = LOCAL_WEIGHT + 1.0 / (ka2 + wb * wb)
            mixed = weight * (wb * out[:, :128] + ka * out[:, 128:])
            q.append(mixed)
            qs.append(pltpu.roll(mixed, 64, 1) * sign)
        rhs = jnp.concatenate([jnp.concatenate(q, 1), jnp.concatenate(qs, 1)], 0)
        back = dot3(pair(w3), split(rhs))
        for j in range(2):
            col = pr * 2 + j
            b = back[:128, j * 128 : (j + 1) * 128]
            bs = back[128:, j * 128 : (j + 1) * 128]
            y = split(b * tw[0] + bs * tw[1])
            for c in range(8):
                at = pl.ds(c * 128 + col * 16, 16)
                yh[at, :] = y[0][c * 16 : c * 16 + 16]
                yl[at, :] = y[1][c * 16 : c * 16 + 16]
    for c in range(8):
        rows = slice(c * 128, (c + 1) * 128)
        out = dot3(pair(e4), (yh[rows, :], yl[rows, :]), True)
        flat[c * 64 : c * 64 + 64, :] = encode(out[:64], out[64:])
        if net and c == 1:
            gather(True)
        if net and c > 0:
            to_col(c - 1, s1, r1, sems[:2])
    if net:
        to_col(COLS - 1, s1, r1, sems[:2])
        own = here()[1]
        r1[own] = s1[own]
        finish(r1, COLS - 1, sems[1])
        to_rows(r1, o, sems[2:])
        finish(s1, COLS - 1, sems[0])
        finish(o, ROWS - 1, sems[2])
    else:
        o[...] = s1[...]


def image_kernel(net, t, f4, m0i, tw, d4, o, s1, r1, vre, vim, *sems):
    if net:
        greet(False)
    flat = s1.reshape(512, 128) if net else s1
    for kg in range(4):
        block = decode(t[pl.ds(kg, 128, stride=4), :])
        lhs = split(jnp.concatenate([part.T for part in block], 1))
        v = dot3(lhs, pair(f4))
        if kg == 0:
            special = dot3((lhs[0][:16], lhs[1][:16]), pair(m0i))
            v = jnp.concatenate([special, v[16:]], 0)
        for col in range(8):
            kk = kg * 8 + col
            re = v[col * 16 : col * 16 + 16, :128]
            im = v[col * 16 : col * 16 + 16, 128:]
            cos = tw[0, kk : kk + 1, :]
            sin = tw[1, kk : kk + 1, :]
            vre[kk * 16 : kk * 16 + 16, :] = re * cos - im * sin
            vim[kk * 16 : kk * 16 + 16, :] = im * cos + re * sin
    for grp in range(4):
        picks = (grp * 2, grp * 2 + 8, grp * 2 + 1, grp * 2 + 9)
        cols = []
        for i in picks:
            at = pl.ds(i, 32, stride=16)
            cols.append(jnp.concatenate([vre[at, :], vim[at, :]], 0))
        out = dot3(pair(d4), split(jnp.concatenate(cols, 1)))
        for j in range(2):
            word = encode(out[:, j * 256 : j * 256 + 128], out[:, j * 256 + 128 : j * 256 + 256])
            flat[pl.ds(grp * 2 + j, 64, stride=8), :] = word
    if net:
        gather(False)
        own = here()[1]
        for i in range(1, COLS):
            to_col(lax.rem(own + i, COLS), s1, r1, sems)
        r1[own] = s1[own]
        finish(r1, COLS - 1, sems[1])
    else:
        r1[...] = s1[...]
    for c in range(8):
        halves = decode(r1[c] if net else r1[c * 64 : c * 64 + 64, :])
        for it in range(2):
            for ph in range(8):
                at = slice(c * 16 + it * 8, c * 16 + it * 8 + 8)
                o[at, ph * 128 : ph * 128 + 128] = halves[it][ph * 8 : ph * 8 + 8]
    if net:
        finish(s1, COLS - 1, sems[0])


def call(kernel, out, scratch, *args, net=None, phases=1, smem=()):
    specs = [
        pl.BlockSpec(memory_space=pltpu.SMEM if i in smem else pltpu.VMEM)
        for i in range(len(args))
    ]
    params = {}
    if net is not None:
        scratch = scratch + [pltpu.SemaphoreType.DMA] * (2 * phases)
        params["compiler_params"] = pltpu.CompilerParams(collective_id=net, has_side_effects=True)
    return pl.pallas_call(
        functools.partial(kernel, net is not None),
        out_shape=jax.ShapeDtypeStruct(*out),
        in_specs=specs,
        out_specs=pl.BlockSpec(memory_space=pltpu.VMEM),
        scratch_shapes=scratch,
        **params,
    )(*args)


def two(table):
    return jnp.asarray(np.stack(table))


def words(*shape):
    return pltpu.VMEM(shape, jnp.int32)


def pull(x, before, after, slopes, tile, rshift, pshift, frac, net=None):
    flip = lambda y: jnp.transpose(y, (0, 2, 1))
    return call(
        pull_kernel,
        ((8, 128, 128), jnp.int32),
        [
            words(8, 128, 128),
            pltpu.VMEM((2, 144, 1024), F32),
            pltpu.VMEM((16, 128), jnp.int32),
            pltpu.VMEM((6, 16, 128), F32),
            pltpu.VMEM((2, 2, 144, 128), F32),
        ],
        x, before, after, slopes, flip(tile), flip(rshift), flip(pshift), flip(frac),
        net=net,
    )


def column_transform(g, net=None):
    t = tables()
    return call(
        column_kernel,
        ((64, 8, 2, 128) if net is not None else (1024, 128), jnp.int32),
        [words(8, 64, 2, 128) if net is not None else words(1024, 128)] * 2 + [pltpu.VMEM((1024, 128), F32)] * 2,
        g, two(t["d1"]), jnp.asarray(t["tw1"]), two(t["f2"]), two(t["m0"]),
        net=net, phases=2,
    )


def row_transform(x, device, net=None):
    t = tables()
    group, low = device // 4, device % 4
    kk = low * 8 + jnp.arange(8, dtype=jnp.int32)
    b = kk + 64 * group + jnp.where((kk == 0) & (group >= 64), 32, 0)
    kb = jnp.where(b > N // 2, b - N, b).astype(F32) * (2.0 * math.pi / N)
    return call(
        row_kernel,
        ((64, 8, 1, 128) if net is not None else (512, 128), jnp.int32),
        [words(8, 64, 1, 128) if net is not None else words(512, 128)] * 2
        + [pltpu.VMEM((2048, 128), BF16)] * 4
        + [pltpu.VMEM((1024, 128), BF16)] * 2,
        kb, x, two(t["e"]), jnp.asarray(t["tw2"]), two(t["w2"]), jnp.asarray(t["ka"]),
        two(t["w3"]), two(t["e4"]),
        smem=(0,), net=net, phases=2,
    )


def image_transform(y, net=None):
    t = tables()
    return call(
        image_kernel,
        ((128, 1024), F32),
        [words(8, 64, 128) if net is not None else words(512, 128)] * 2 + [pltpu.VMEM((512, 128), F32)] * 2,
        y, two(t["f4"]), two(t["m0i"]), jnp.asarray(t["tw1"]), two(t["d4"]),
        net=net,
    )


def per_device(residual, field_slopes, source_tile, row_shift, pixel_shift, fraction):
    peers = lax.axis_size("rows")
    up = [(i, i + 1) for i in range(peers - 1)]
    down = [(j, i) for i, j in up]
    before = lax.ppermute(residual[:, -HALO:], "rows", up)
    after = lax.ppermute(residual[:, :HALO], "rows", down)
    flow = pull(
        residual, before, after, field_slopes, source_tile, row_shift, pixel_shift, fraction,
        net=0,
    )
    spectra = column_transform(flow.reshape(1024, 128), net=1)
    device = lax.axis_index("rows") * lax.axis_size("cols") + lax.axis_index("cols")
    mixed = row_transform(spectra.reshape(1024, 128), device, net=2)
    return image_transform(mixed.reshape(512, 128), net=3)


def solution(mesh):
    spec = P(None, "rows", "cols")
    return jax.shard_map(
        per_device,
        mesh=mesh,
        in_specs=(spec,) * 6,
        out_specs=P("rows", "cols"),
        check_vma=False,
    )
```

```python
import functools
import math

import jax
import jax.numpy as jnp
import ml_dtypes
import numpy as np
from jax import lax
from jax.experimental import pallas as pl
from jax.experimental.pallas import tpu as pltpu
from jax.sharding import PartitionSpec as P

N = 8192
TILE = 128
HALO = 8
SHIFT = 2
LOCAL_WEIGHT = 0.5
FLOOR = 8.0 * math.pi / N

F32 = jnp.float32
BF16 = jnp.bfloat16
TINY = 1e-18
BIAS = 120.0
STEPS = 16380.0
CENTRE = 16384.0


def split_table(x):
    hi = x.astype(ml_dtypes.bfloat16)
    lo = (x - hi.astype(np.float64)).astype(ml_dtypes.bfloat16)
    return hi, lo


def cs(angle):
    return np.cos(angle), np.sin(angle)


@functools.lru_cache(maxsize=None)
def tables():
    two_pi = 2.0 * np.pi
    t = {}
    p = np.arange(64)[None, :]
    kk = np.arange(32)[:, None]
    c, s = cs(two_pi * ((p * kk) % 64) / 64)
    d1 = np.concatenate([c, -s], 0)
    d1[32] = (-1.0) ** np.arange(64)
    t["d1"] = split_table(d1)
    d4 = np.concatenate([2 * c, -2 * s], 0).T.copy()
    d4[:, 0] = 1.0
    d4[:, 32] = (-1.0) ** np.arange(64)
    t["d4"] = split_table(d4 / (N * N))
    q = np.arange(128)[None, :]
    c, s = cs(two_pi * (kk * q) / N)
    t["tw1"] = np.stack([c, s]).astype(np.float32)
    l = np.arange(128)[:, None]
    c, s = cs(two_pi * ((l * q) % 128) / 128)
    f2 = np.block([[c, s], [-s, c]])
    order = np.concatenate([np.arange(0, 128, 2), np.arange(1, 128, 2)])
    order = np.concatenate([order, 128 + order])
    t["f2"] = split_table(f2[order])
    t["f4"] = split_table(np.block([[c, s], [-s, c]]))
    c32, s32 = cs(two_pi * ((q * (32 + 64 * l)) % N) / N)
    low = l < 64
    alt = np.broadcast_to((-1.0) ** q, (1, 128))
    m0 = np.zeros((256, 256))
    m0[:128, :128] = np.where(low, c, 0.0)
    m0[128:, :128] = np.where(low, -s, 0.0)
    m0[128:129, :128] = alt
    m0[:128, 128:] = np.where(low, 0.0, c32)
    m0[128:, 128:] = np.where(low, 0.0, -s32)
    t["m0"] = split_table(m0[order])
    mi = 2.0 * m0
    mi[0] *= 0.5
    mi[128] *= 0.5
    t["m0i"] = split_table(mi)
    r = np.arange(64)[:, None]
    m = np.arange(64)[None, :]
    c, s = cs(two_pi * ((r * m) % 64) / 64)
    e_re = np.concatenate([c, s], 0)
    e_im = np.concatenate([-s, c], 0)
    t["e"] = split_table(np.concatenate([e_re, e_im, -e_im, e_re], 1))
    t["e4"] = split_table(np.block([[c, -s], [s, c]]))
    q2 = np.arange(128)[:, None]
    mm = np.concatenate([np.arange(64), np.arange(64)])[None, :]
    c, s = cs(two_pi * (q2 * mm) / N)
    t["tw2"] = np.stack([c, s]).astype(np.float32)
    n = np.arange(128)[:, None]
    c, s = cs(two_pi * ((n * q2.T) % 128) / 128)
    t["w2"] = split_table(np.concatenate([c, -s], 1))
    t["w3"] = split_table(np.block([[s, -c], [c, s]]))
    a = mm + 64 * n
    signed = np.where(a > N // 2, a - N, np.where(a == N // 2, 0, a))
    t["ka"] = (signed * (two_pi / N)).astype(np.float32)
    return t


def split(x):
    hi = x.astype(BF16)
    return hi, (x - hi.astype(F32)).astype(BF16)


def dot(a, b, transposed=False):
    dims = (((1,), (1 if transposed else 0,)), ((), ()))
    return lax.dot_general(a, b, dims, preferred_element_type=F32)


def dot3(a, b, transposed=False):
    (ah, al), (bh, bl) = a, b
    return dot(ah, bh, transposed) + (dot(ah, bl, transposed) + dot(al, bh, transposed))


def pair(ref):
    return ref[0], ref[1]


MESH = pl.DeviceIdType.MESH
ROWS, COLS = 64, 8


def here():
    return lax.axis_index("rows"), lax.axis_index("cols")


def div(a, n):
    return a // n if isinstance(a, int) else lax.div(a, jnp.int32(n))


def rem(a, n):
    return a % n if isinstance(a, int) else lax.rem(a, jnp.int32(n))


def place():
    r, c = here()
    return rem(c, 4), div(r, 16) * 2 + div(c, 4), rem(div(r, 2), 8), rem(r, 2)


def at_place(x, y, z, core):
    return div(y, 2) * 16 + z * 2 + core, rem(y, 2) * 4 + x


DY_ORDER = (1, 7, 2, 6, 3, 5, 4, 0)
OFFSETS = tuple(
    (dy, (q + k) % 8, core)
    for core in range(2)
    for q in range(8)
    for k, dy in enumerate(DY_ORDER)
    if (dy, (q + k) % 8, core) != (0, 0, 0)
)


def signal(peer):
    barrier = pltpu.get_barrier_semaphore()
    pl.semaphore_signal(barrier, inc=1, device_id=peer, device_id_type=MESH)


def greet_cols():
    r, c = here()
    for i in range(1, COLS):
        signal((r, lax.rem(c + i, COLS)))


def greet_plane(part):
    x, y, z, core = place()
    if part == 0:
        for i in range(1, 4):
            signal(at_place(rem(x + i, 4), y, z, core))
    for dy, dz, dc in OFFSETS[part::8]:
        signal(at_place(x, rem(y + dy, 8), rem(z + dz, 8), rem(core + dc, 2)))


def gather(count):
    pl.semaphore_wait(pltpu.get_barrier_semaphore(), count)


PLANE = 3 + len(OFFSETS)


def remote(src, dst, sems, peer):
    pltpu.make_async_remote_copy(
        src_ref=src,
        dst_ref=dst,
        send_sem=sems[0],
        recv_sem=sems[1],
        device_id=peer,
        device_id_type=MESH,
    ).start()


def to_col(peer, src, dst, sems):
    r, c = here()

    @pl.when(peer != c)
    def _():
        remote(src.at[peer], dst.at[c], sems, (r, peer))


def to_x(peer, src, dst, send, near, far):
    x, y, z, core = place()
    partner = x + 1 - 2 * rem(x, 2)

    @pl.when(peer == partner)
    def _():
        remote(src.at[peer], dst.at[x], (send, near), at_place(peer, y, z, core))

    @pl.when(div(peer, 2) != div(x, 2))
    def _():
        remote(src.at[peer], dst.at[x], (send, far), at_place(peer, y, z, core))


def finish(ref, count, sem):
    part = ref.at[pl.ds(0, count)]
    pltpu.make_async_copy(part, part, sem).wait()


def exchange_plane(s1, r1, o, sems):
    x, y, z, core = place()
    r, c = here()
    send1, near, far, send2, recv2 = sems
    r1[x] = s1[x]
    for step in range(2):
        finish(r1, 1 + step, (near, far)[step])
        first = 2 * rem(div(x, 2) + step, 2)
        planes = [rem(y + dy, 8) for dy in DY_ORDER]
        bases = [(div(yy, 2) * 16, rem(yy, 2)) for yy in planes]
        mine = o.at[r, pl.ds(rem(y, 2) * 4 + first, 2)]

        def row(q, _):
            dc = div(q, 8)
            side = rem(core + dc, 2)
            for k, dy in enumerate(DY_ORDER):
                dz = rem(q + k, 8)
                line = bases[k][0] + rem(z + dz, 8) * 2 + side
                half = bases[k][1]

                def go():
                    remote(
                        r1.at[pl.ds(first, 2), half * 64 + line],
                        mine,
                        (send2, recv2),
                        (line, half * 4 + x),
                    )

                if dy == 0:
                    pl.when(dz + dc > 0)(go)
                else:
                    go()
            return 0

        lax.fori_loop(0, 16, row, 0)
    o[r, pl.ds(rem(y, 2) * 4, 4)] = r1[:, rem(y, 2) * 64 + r]
    finish(s1, 3, send1)
    part = s1.at[:, pl.ds(0, 127)]
    pltpu.make_async_copy(part, part, recv2).wait()
    pltpu.make_async_copy(part, part, send2).wait()


def spread(x, join):
    x = join(x, pltpu.roll(x, 64, 1))
    return join(x, pltpu.roll(x, 32, 1))


def lane_field(shape):
    return lax.shift_left(
        lax.shift_right_logical(lax.broadcasted_iota(jnp.int32, shape, 1), 5), 1
    )


def encode(x, y):
    peak = spread(jnp.maximum(jnp.abs(x), jnp.abs(y)), jnp.maximum)
    level = jnp.ceil(2.0 * jnp.log2(jnp.maximum(peak, TINY))) + BIAS
    level = jnp.clip(level, 0.0, 255.0)
    gain = jnp.exp2((BIAS - level) * 0.5) * STEPS
    code = level.astype(jnp.int32)
    bits = lax.shift_right_logical(code, lane_field(x.shape)) & 3
    qx = (x * gain + (CENTRE + 0.5)).astype(jnp.int32)
    qy = (y * gain + (CENTRE + 0.5)).astype(jnp.int32)
    return qx | lax.shift_left(qy, 15) | lax.shift_left(bits, 30)


def decode(word):
    bits = lax.shift_right_logical(word, 30) & 3
    code = spread(lax.shift_left(bits, lane_field(word.shape)), jnp.add)
    scale = jnp.exp2((code.astype(F32) - BIAS) * 0.5) * (1.0 / STEPS)
    x = (word & 32767).astype(F32) - CENTRE
    y = (lax.shift_right_logical(word, 15) & 32767).astype(F32) - CENTRE
    return x * scale, y * scale


def pull_kernel(net, x, before, after, slopes, tile, rshift, pshift, frac, o, s1, padded, spots, wts, sc, *sems):
    own = here()[1] if net else 0
    if net:
        greet_cols()
    padded[:, 0:HALO, :] = before[...].astype(F32)
    padded[:, HALO : HALO + 128, :] = x[...].astype(F32)
    padded[:, HALO + 128 :, :] = after[...].astype(F32)
    sc[:, :, 0:8, :] = jnp.zeros((2, 2, 8, 128), F32)
    sc[:, :, 136:144, :] = jnp.zeros((2, 2, 8, 128), F32)
    lane = lax.broadcasted_iota(jnp.int32, (8, 128), 1)

    def by_block(values):
        out = jnp.zeros((8, 128), values.dtype)
        for t in range(8):
            row = jnp.broadcast_to(values[t : t + 1, :], (8, 128))
            row = pltpu.roll(pltpu.roll(row, (16 * t + 16) % 128, 1), 0, 1, stride=16, stride_axis=0)
            out = jnp.where((lane >= 16 * t) & (lane < 16 * t + 16), row, out)
        return out

    for k in range(2):
        rows = slice(k * 8, k * 8 + 8)
        index = tile[k] * 32 + (lax.rem(lane, 16) + HALO) + rshift[k]
        spots[rows, :] = by_block(index)
        ps = by_block(pshift[k])
        f = by_block(frac[k])
        for oi in range(6):
            off = oi - SHIFT
            wts[oi, rows, :] = jnp.where(ps == off, 1.0 - f, 0.0) + jnp.where(
                ps + 1 == off, f, 0.0
            )
    place = lax.broadcasted_iota(jnp.int32, (256, 128), 0)

    def block(n, _):
        b = lax.rem(own + 1 + n, COLS)
        r0 = pl.multiple_of(b * 16, 16)
        window = [
            jnp.concatenate(
                [padded[p, pl.ds(r0, 32), u * 128 : (u + 1) * 128] for u in range(8)], 0
            )
            for p in range(2)
        ]
        window = jnp.concatenate(window, 1).astype(BF16)
        hot = jnp.concatenate(
            [
                jnp.where(place == spots[pl.ds(k * 8 + 7 - b, 1), :], 1.0, 0.0).astype(BF16)
                for k in range(2)
            ],
            1,
        )
        picked = lax.dot_general(
            window, hot, (((0,), (0,)), ((), ())), preferred_element_type=F32
        )
        for p in range(2):
            for k in range(2):
                sc[p, k, 8:136, :] = picked[p * 128 : p * 128 + 128, k * 128 : k * 128 + 128]
        got = []
        for p in range(2):
            total = None
            for oi in range(6):
                for k in range(2):
                    w = wts[oi, pl.ds(k * 8 + 7 - b, 1), :]
                    part = w * sc[p, k, 8 + oi - SHIFT : 136 + oi - SHIFT, :]
                    total = part if total is None else total + part
            got.append(total.T)
        for t in range(8):
            at = slice(t * 16, t * 16 + 16)
            first, second = got[0][at], got[1][at]
            s = [slopes[i, pl.ds(r0, 16), t * 128 : (t + 1) * 128].astype(F32) for i in range(4)]
            across = -(first * s[0] + second * s[1])
            down = -(first * s[2] + second * s[3])
            s1[b, t * 16 : t * 16 + 16, :] = encode(across, down)
        if net:

            @pl.when(n == 1)
            def _():
                gather(COLS - 1)

            @pl.when(n > 0)
            def _():
                to_col(lax.rem(own + n, COLS), s1, o, sems)

        return 0

    lax.fori_loop(0, 8, block, 0)
    if net:
        o[own] = s1[own]
        finish(o, COLS - 1, sems[1])
        finish(s1, COLS - 1, sems[0])
    else:
        o[...] = s1[...]


def column_kernel(net, g, d1, tw, f2, m0, o, s1, r1, ure, uim, *sems):
    flat = s1.reshape(1024, 128) if net else s1
    cos, sin = tw[0], tw[1]
    for grp in range(8):
        if net:
            greet_plane(grp)
        x, at = [], []
        for i in (2 * grp, 2 * grp + 1):
            x += decode(g[pl.ds(i, 64, stride=16), :])
            at += [i, 16 + i]
        v = dot3(pair(d1), split(jnp.concatenate(x, 1)))
        for j in range(4):
            re = v[:32, j * 128 : (j + 1) * 128]
            im = v[32:, j * 128 : (j + 1) * 128]
            ure[pl.ds(at[j], 32, stride=32), :] = re * cos + im * sin
            uim[pl.ds(at[j], 32, stride=32), :] = im * cos - re * sin
    lane = lax.broadcasted_iota(jnp.int32, (256, 128), 1)

    def send(kg):
        if net and kg >= 0:
            if kg == 0:
                gather(PLANE)
            to_x(kg, s1, r1, *sems[:3])

    for kg in range(4):
        rows = slice(kg * 256, (kg + 1) * 256)
        rhs = split(jnp.concatenate([ure[rows, :], uim[rows, :]], 1))
        out = dot3(pair(f2), rhs, True)
        for h in range(2):
            part = out[:, h * 128 : (h + 1) * 128]
            if kg == 0 and h == 0:
                special = dot3(pair(m0), (rhs[0][:128], rhs[1][:128]), True)
                part = jnp.where(lane < 32, special, part)
            word = encode(part[:128], part[128:])
            for half in range(2):
                at = pl.ds((kg * 2 + half) * 128 + h, 64, stride=2)
                flat[at, :] = word[half * 64 : half * 64 + 64]
        send(kg - 1)
    send(3)
    if net:
        exchange_plane(s1, r1, o, sems)
    else:
        o[...] = s1[...]


def row_kernel(net, kb, x, e, tw, w2, ka_ref, w3, e4, o, s1, r1, uh, ul, sh, sl, yh, yl, *sems):
    flat = s1.reshape(512, 128) if net else s1
    for c in range(8):
        if net:
            greet_plane(c)
        cos = jnp.concatenate([tw[0, c * 16 : c * 16 + 16, :]] * 8, 0)
        sin = jnp.concatenate([tw[1, c * 16 : c * 16 + 16, :]] * 8, 0)
        for h in range(2):
            block = jnp.concatenate(decode(x[pl.ds(c * 2 + h, 64, stride=16), :]), 0)
            both = dot3(split(block.T), pair(e))
            v, vs = both[:, :128], both[:, 128:]
            u = split(v * cos - vs * sin)
            us = split(vs * cos + v * sin)
            for kf in range(8):
                at = pl.ds((h * 8 + kf) * 128 + c * 16, 16)
                part = slice(kf * 16, kf * 16 + 16)
                uh[at, :] = u[0][part]
                ul[at, :] = u[1][part]
                sh[at, :] = us[0][part]
                sl[at, :] = us[1][part]
    ka = ka_ref[...]
    ka2 = ka * ka + FLOOR * FLOOR
    sign = jnp.where(lax.broadcasted_iota(jnp.int32, (128, 128), 1) < 64, -1.0, 1.0)

    def stack(first, second, col):
        parts = []
        for f in range(2):
            at = slice((col * 2 + f) * 128, (col * 2 + f + 1) * 128)
            parts.append(jnp.concatenate([first[at, :], second[at, :]], 0))
        return jnp.concatenate(parts, 1)

    for pr in range(4):
        q, qs = [], []
        for j in range(2):
            col = pr * 2 + j
            out = dot3(pair(w2), (stack(uh, sh, col), stack(ul, sl, col)))
            wb = kb[col]
            weight = LOCAL_WEIGHT + 1.0 / (ka2 + wb * wb)
            mixed = weight * (wb * out[:, :128] + ka * out[:, 128:])
            q.append(mixed)
            qs.append(pltpu.roll(mixed, 64, 1) * sign)
        rhs = jnp.concatenate([jnp.concatenate(q, 1), jnp.concatenate(qs, 1)], 0)
        back = dot3(pair(w3), split(rhs))
        for j in range(2):
            col = pr * 2 + j
            b = back[:128, j * 128 : (j + 1) * 128]
            bs = back[128:, j * 128 : (j + 1) * 128]
            y = split(b * tw[0] + bs * tw[1])
            for c in range(8):
                at = pl.ds(c * 128 + col * 16, 16)
                yh[at, :] = y[0][c * 16 : c * 16 + 16]
                yl[at, :] = y[1][c * 16 : c * 16 + 16]
    for peer in range(4):
        for half in range(2):
            c = half * 4 + peer
            rows = slice(c * 128, (c + 1) * 128)
            out = dot3(pair(e4), (yh[rows, :], yl[rows, :]), True)
            at = (peer * 2 + half) * 64
            flat[at : at + 64, :] = encode(out[:64], out[64:])
        if net and peer == 1:
            gather(PLANE)
        if net and peer > 0:
            to_x(peer - 1, s1, r1, *sems[:3])
    if net:
        to_x(3, s1, r1, *sems[:3])
        exchange_plane(s1, r1, o, sems)
    else:
        o[...] = s1[...]


def image_kernel(net, t, f4, m0i, tw, d4, o, s1, r1, vre, vim, *sems):
    if net:
        greet_cols()
    flat = s1.reshape(512, 128) if net else s1
    for kg in range(4):
        block = decode(t[pl.ds(kg, 128, stride=4), :])
        lhs = split(jnp.concatenate([part.T for part in block], 1))
        v = dot3(lhs, pair(f4))
        if kg == 0:
            special = dot3((lhs[0][:16], lhs[1][:16]), pair(m0i))
            v = jnp.concatenate([special, v[16:]], 0)
        for col in range(8):
            kk = kg * 8 + col
            re = v[col * 16 : col * 16 + 16, :128]
            im = v[col * 16 : col * 16 + 16, 128:]
            cos = tw[0, kk : kk + 1, :]
            sin = tw[1, kk : kk + 1, :]
            vre[kk * 16 : kk * 16 + 16, :] = re * cos - im * sin
            vim[kk * 16 : kk * 16 + 16, :] = im * cos + re * sin
    for grp in range(4):
        picks = (grp * 2, grp * 2 + 8, grp * 2 + 1, grp * 2 + 9)
        cols = []
        for i in picks:
            at = pl.ds(i, 32, stride=16)
            cols.append(jnp.concatenate([vre[at, :], vim[at, :]], 0))
        out = dot3(pair(d4), split(jnp.concatenate(cols, 1)))
        for j in range(2):
            word = encode(out[:, j * 256 : j * 256 + 128], out[:, j * 256 + 128 : j * 256 + 256])
            flat[pl.ds(grp * 2 + j, 64, stride=8), :] = word
    if net:
        gather(COLS - 1)
        own = here()[1]
        for i in range(1, COLS):
            to_col(lax.rem(own + i, COLS), s1, r1, sems)
        r1[own] = s1[own]
        finish(r1, COLS - 1, sems[1])
    else:
        r1[...] = s1[...]
    for c in range(8):
        halves = decode(r1[c] if net else r1[c * 64 : c * 64 + 64, :])
        for it in range(2):
            for ph in range(8):
                at = slice(c * 16 + it * 8, c * 16 + it * 8 + 8)
                o[at, ph * 128 : ph * 128 + 128] = halves[it][ph * 8 : ph * 8 + 8]
    if net:
        finish(s1, COLS - 1, sems[0])


def call(kernel, out, scratch, *args, net=None, phases=2, smem=()):
    specs = [
        pl.BlockSpec(memory_space=pltpu.SMEM if i in smem else pltpu.VMEM)
        for i in range(len(args))
    ]
    params = {}
    if net is not None:
        scratch = scratch + [pltpu.SemaphoreType.DMA] * phases
        params["compiler_params"] = pltpu.CompilerParams(collective_id=net, has_side_effects=True)
    return pl.pallas_call(
        functools.partial(kernel, net is not None),
        out_shape=jax.ShapeDtypeStruct(*out),
        in_specs=specs,
        out_specs=pl.BlockSpec(memory_space=pltpu.VMEM),
        scratch_shapes=scratch,
        **params,
    )(*args)


def two(table):
    return jnp.asarray(np.stack(table))


def words(*shape):
    return pltpu.VMEM(shape, jnp.int32)


def pull(x, before, after, slopes, tile, rshift, pshift, frac, net=None):
    flip = lambda y: jnp.transpose(y, (0, 2, 1))
    return call(
        pull_kernel,
        ((8, 128, 128), jnp.int32),
        [
            words(8, 128, 128),
            pltpu.VMEM((2, 144, 1024), F32),
            pltpu.VMEM((16, 128), jnp.int32),
            pltpu.VMEM((6, 16, 128), F32),
            pltpu.VMEM((2, 2, 144, 128), F32),
        ],
        x, before, after, slopes, flip(tile), flip(rshift), flip(pshift), flip(frac),
        net=net,
    )


def column_transform(g, net=None):
    t = tables()
    return call(
        column_kernel,
        ((64, 8, 2, 128) if net is not None else (1024, 128), jnp.int32),
        [words(4, 128, 2, 128) if net is not None else words(1024, 128)] * 2 + [pltpu.VMEM((1024, 128), F32)] * 2,
        g, two(t["d1"]), jnp.asarray(t["tw1"]), two(t["f2"]), two(t["m0"]),
        net=net, phases=5,
    )


def row_transform(x, device, net=None):
    t = tables()
    group, low = device // 4, device % 4
    kk = low * 8 + jnp.arange(8, dtype=jnp.int32)
    b = kk + 64 * group + jnp.where((kk == 0) & (group >= 64), 32, 0)
    kb = jnp.where(b > N // 2, b - N, b).astype(F32) * (2.0 * math.pi / N)
    return call(
        row_kernel,
        ((64, 8, 1, 128) if net is not None else (512, 128), jnp.int32),
        [words(4, 128, 1, 128) if net is not None else words(512, 128)] * 2
        + [pltpu.VMEM((2048, 128), BF16)] * 4
        + [pltpu.VMEM((1024, 128), BF16)] * 2,
        kb, x, two(t["e"]), jnp.asarray(t["tw2"]), two(t["w2"]), jnp.asarray(t["ka"]),
        two(t["w3"]), two(t["e4"]),
        smem=(0,), net=net, phases=5,
    )


def image_transform(y, net=None):
    t = tables()
    return call(
        image_kernel,
        ((128, 1024), F32),
        [words(8, 64, 128) if net is not None else words(512, 128)] * 2 + [pltpu.VMEM((512, 128), F32)] * 2,
        y, two(t["f4"]), two(t["m0i"]), jnp.asarray(t["tw1"]), two(t["d4"]),
        net=net,
    )


def per_device(residual, field_slopes, source_tile, row_shift, pixel_shift, fraction):
    peers = lax.axis_size("rows")
    up = [(i, i + 1) for i in range(peers - 1)]
    down = [(j, i) for i, j in up]
    before = lax.ppermute(residual[:, -HALO:], "rows", up)
    after = lax.ppermute(residual[:, :HALO], "rows", down)
    flow = pull(
        residual, before, after, field_slopes, source_tile, row_shift, pixel_shift, fraction,
        net=0,
    )
    spectra = column_transform(flow.reshape(1024, 128), net=1)
    device = lax.axis_index("rows") * lax.axis_size("cols") + lax.axis_index("cols")
    mixed = row_transform(spectra.reshape(1024, 128), device, net=2)
    return image_transform(mixed.reshape(512, 128), net=3)


def solution(mesh):
    spec = P(None, "rows", "cols")
    return jax.shard_map(
        per_device,
        mesh=mesh,
        in_specs=(spec,) * 6,
        out_specs=P("rows", "cols"),
        check_vma=False,
    )
```

```python
import functools
import math

import jax
import jax.numpy as jnp
import ml_dtypes
import numpy as np
from jax import lax
from jax.experimental import pallas as pl
from jax.experimental.pallas import tpu as pltpu
from jax.sharding import PartitionSpec as P

N = 8192
TILE = 128
HALO = 8
SHIFT = 2
LOCAL_WEIGHT = 0.5
FLOOR = 8.0 * math.pi / N

F32 = jnp.float32
BF16 = jnp.bfloat16
TINY = 1e-18
BIAS = 120.0
STEPS = 16380.0
CENTRE = 16384.0


def split_table(x):
    hi = x.astype(ml_dtypes.bfloat16)
    lo = (x - hi.astype(np.float64)).astype(ml_dtypes.bfloat16)
    return hi, lo


def cs(angle):
    return np.cos(angle), np.sin(angle)


@functools.lru_cache(maxsize=None)
def tables():
    two_pi = 2.0 * np.pi
    t = {}
    p = np.arange(64)[None, :]
    kk = np.arange(32)[:, None]
    c, s = cs(two_pi * ((p * kk) % 64) / 64)
    d1 = np.concatenate([c, -s], 0)
    d1[32] = (-1.0) ** np.arange(64)
    t["d1"] = split_table(d1)
    d4 = np.concatenate([2 * c, -2 * s], 0).T.copy()
    d4[:, 0] = 1.0
    d4[:, 32] = (-1.0) ** np.arange(64)
    t["d4"] = split_table(d4 / (N * N))
    q = np.arange(128)[None, :]
    c, s = cs(two_pi * (kk * q) / N)
    t["tw1"] = np.stack([c, s]).astype(np.float32)
    l = np.arange(128)[:, None]
    c, s = cs(two_pi * ((l * q) % 128) / 128)
    f2 = np.block([[c, s], [-s, c]])
    order = np.concatenate([np.arange(0, 128, 2), np.arange(1, 128, 2)])
    order = np.concatenate([order, 128 + order])
    t["f2"] = split_table(f2[order])
    t["f4"] = split_table(np.block([[c, s], [-s, c]]))
    c32, s32 = cs(two_pi * ((q * (32 + 64 * l)) % N) / N)
    low = l < 64
    alt = np.broadcast_to((-1.0) ** q, (1, 128))
    m0 = np.zeros((256, 256))
    m0[:128, :128] = np.where(low, c, 0.0)
    m0[128:, :128] = np.where(low, -s, 0.0)
    m0[128:129, :128] = alt
    m0[:128, 128:] = np.where(low, 0.0, c32)
    m0[128:, 128:] = np.where(low, 0.0, -s32)
    t["m0"] = split_table(m0[order])
    mi = 2.0 * m0
    mi[0] *= 0.5
    mi[128] *= 0.5
    t["m0i"] = split_table(mi)
    r = np.arange(64)[:, None]
    m = np.arange(64)[None, :]
    c, s = cs(two_pi * ((r * m) % 64) / 64)
    e_re = np.concatenate([c, s], 0)
    e_im = np.concatenate([-s, c], 0)
    t["e"] = split_table(np.concatenate([e_re, e_im, -e_im, e_re], 1))
    t["e4"] = split_table(np.block([[c, -s], [s, c]]))
    q2 = np.arange(128)[:, None]
    mm = np.concatenate([np.arange(64), np.arange(64)])[None, :]
    c, s = cs(two_pi * (q2 * mm) / N)
    t["tw2"] = np.stack([c, s]).astype(np.float32)
    n = np.arange(128)[:, None]
    c, s = cs(two_pi * ((n * q2.T) % 128) / 128)
    t["w2"] = split_table(np.concatenate([c, -s], 1))
    t["w3"] = split_table(np.block([[s, -c], [c, s]]))
    a = mm + 64 * n
    signed = np.where(a > N // 2, a - N, np.where(a == N // 2, 0, a))
    t["ka"] = (signed * (two_pi / N)).astype(np.float32)
    return t


def split(x):
    hi = x.astype(BF16)
    return hi, (x - hi.astype(F32)).astype(BF16)


def dot(a, b, transposed=False):
    dims = (((1,), (1 if transposed else 0,)), ((), ()))
    return lax.dot_general(a, b, dims, preferred_element_type=F32)


def dot3(a, b, transposed=False):
    (ah, al), (bh, bl) = a, b
    return dot(ah, bh, transposed) + (dot(ah, bl, transposed) + dot(al, bh, transposed))


def pair(ref):
    return ref[0], ref[1]


MESH = pl.DeviceIdType.MESH
ROWS, COLS = 64, 8


def here():
    return lax.axis_index("rows"), lax.axis_index("cols")


def greet():
    r, c = here()
    barrier = pltpu.get_barrier_semaphore()
    for i in range(1, COLS):
        peer = (r, lax.rem(c + i, COLS))
        pl.semaphore_signal(barrier, inc=1, device_id=peer, device_id_type=MESH)

    def signal(i, _):
        peer = (lax.rem(r + i, ROWS), c)
        pl.semaphore_signal(barrier, inc=1, device_id=peer, device_id_type=MESH)
        return 0

    lax.fori_loop(1, ROWS, signal, 0)


def gather():
    pl.semaphore_wait(pltpu.get_barrier_semaphore(), COLS - 1 + ROWS - 1)


def remote(src, dst, sems, peer):
    pltpu.make_async_remote_copy(
        src_ref=src,
        dst_ref=dst,
        send_sem=sems[0],
        recv_sem=sems[1],
        device_id=peer,
        device_id_type=MESH,
    ).start()


def to_col(peer, src, dst, send, near, far):
    r, c = here()
    same = lax.div(c, 4) == peer // 4 if isinstance(peer, int) else lax.div(c, 4) == lax.div(peer, 4)

    @pl.when(same & (peer != c))
    def _():
        remote(src.at[peer], dst.at[c], (send, near), (r, peer))

    @pl.when(jnp.logical_not(same))
    def _():
        remote(src.at[peer], dst.at[c], (send, far), (r, peer))


def finish(ref, count, sem):
    part = ref.at[pl.ds(0, count)]
    pltpu.make_async_copy(part, part, sem).wait()


def to_rows(src, dst, sems, first, count):
    r, c = here()

    def send(i, _):
        peer = lax.rem(r + lax.rem(i * 27, ROWS), ROWS)
        remote(
            src.at[pl.ds(first, count), peer], dst.at[r, pl.ds(first, count)], sems, (peer, c)
        )
        return 0

    lax.fori_loop(1, ROWS, send, 0)


def all_exchange(s1, r1, o, sems, split_groups):
    send1, near, far, send2, recv2 = sems
    r, c = here()
    r1[c] = s1[c]
    own = lax.div(c, 4) * 4
    finish(r1, 3, near)
    if split_groups:
        to_rows(r1, o, (send2, recv2), own, 4)
        finish(r1, 4, far)
        to_rows(r1, o, (send2, recv2), 4 - own, 4)
    else:
        finish(r1, 4, far)
        to_rows(r1, o, (send2, recv2), 0, 8)
    o[r] = r1[:, r]
    finish(o, ROWS - 1, recv2)
    finish(s1, COLS - 1, send1)
    finish(o, ROWS - 1, send2)


def spread(x, join):
    x = join(x, pltpu.roll(x, 64, 1))
    return join(x, pltpu.roll(x, 32, 1))


def lane_field(shape):
    return lax.shift_left(
        lax.shift_right_logical(lax.broadcasted_iota(jnp.int32, shape, 1), 5), 1
    )


def encode(x, y):
    peak = spread(jnp.maximum(jnp.abs(x), jnp.abs(y)), jnp.maximum)
    level = jnp.ceil(2.0 * jnp.log2(jnp.maximum(peak, TINY))) + BIAS
    level = jnp.clip(level, 0.0, 255.0)
    gain = jnp.exp2((BIAS - level) * 0.5) * STEPS
    code = level.astype(jnp.int32)
    bits = lax.shift_right_logical(code, lane_field(x.shape)) & 3
    qx = (x * gain + (CENTRE + 0.5)).astype(jnp.int32)
    qy = (y * gain + (CENTRE + 0.5)).astype(jnp.int32)
    return qx | lax.shift_left(qy, 15) | lax.shift_left(bits, 30)


def decode(word):
    bits = lax.shift_right_logical(word, 30) & 3
    code = spread(lax.shift_left(bits, lane_field(word.shape)), jnp.add)
    scale = jnp.exp2((code.astype(F32) - BIAS) * 0.5) * (1.0 / STEPS)
    x = (word & 32767).astype(F32) - CENTRE
    y = (lax.shift_right_logical(word, 15) & 32767).astype(F32) - CENTRE
    return x * scale, y * scale


def pull_kernel(net, x, before, after, slopes, tile, rshift, pshift, frac, o, s1, padded, spots, wts, sc, *sems):
    own = here()[1] if net else 0
    padded[:, 0:HALO, :] = before[...].astype(F32)
    padded[:, HALO : HALO + 128, :] = x[...].astype(F32)
    padded[:, HALO + 128 :, :] = after[...].astype(F32)
    sc[:, :, 0:8, :] = jnp.zeros((2, 2, 8, 128), F32)
    sc[:, :, 136:144, :] = jnp.zeros((2, 2, 8, 128), F32)
    lane = lax.broadcasted_iota(jnp.int32, (8, 128), 1)

    def by_block(values):
        out = jnp.zeros((8, 128), values.dtype)
        for t in range(8):
            row = jnp.broadcast_to(values[t : t + 1, :], (8, 128))
            row = pltpu.roll(pltpu.roll(row, (16 * t + 16) % 128, 1), 0, 1, stride=16, stride_axis=0)
            out = jnp.where((lane >= 16 * t) & (lane < 16 * t + 16), row, out)
        return out

    for k in range(2):
        rows = slice(k * 8, k * 8 + 8)
        index = tile[k] * 32 + (lax.rem(lane, 16) + HALO) + rshift[k]
        spots[rows, :] = by_block(index)
        ps = by_block(pshift[k])
        f = by_block(frac[k])
        for oi in range(6):
            off = oi - SHIFT
            wts[oi, rows, :] = jnp.where(ps == off, 1.0 - f, 0.0) + jnp.where(
                ps + 1 == off, f, 0.0
            )
    place = lax.broadcasted_iota(jnp.int32, (256, 128), 0)

    def block(n, _):
        b = lax.rem(own + 1 + n, COLS)
        r0 = pl.multiple_of(b * 16, 16)
        window = [
            jnp.concatenate(
                [padded[p, pl.ds(r0, 32), u * 128 : (u + 1) * 128] for u in range(8)], 0
            )
            for p in range(2)
        ]
        window = jnp.concatenate(window, 1).astype(BF16)
        hot = jnp.concatenate(
            [
                jnp.where(place == spots[pl.ds(k * 8 + 7 - b, 1), :], 1.0, 0.0).astype(BF16)
                for k in range(2)
            ],
            1,
        )
        picked = lax.dot_general(
            window, hot, (((0,), (0,)), ((), ())), preferred_element_type=F32
        )
        for p in range(2):
            for k in range(2):
                sc[p, k, 8:136, :] = picked[p * 128 : p * 128 + 128, k * 128 : k * 128 + 128]
        got = []
        for p in range(2):
            total = None
            for oi in range(6):
                for k in range(2):
                    w = wts[oi, pl.ds(k * 8 + 7 - b, 1), :]
                    part = w * sc[p, k, 8 + oi - SHIFT : 136 + oi - SHIFT, :]
                    total = part if total is None else total + part
            got.append(total.T)
        for t in range(8):
            at = slice(t * 16, t * 16 + 16)
            first, second = got[0][at], got[1][at]
            s = [slopes[i, pl.ds(r0, 16), t * 128 : (t + 1) * 128].astype(F32) for i in range(4)]
            across = -(first * s[0] + second * s[1])
            down = -(first * s[2] + second * s[3])
            s1[b, t * 16 : t * 16 + 16, :] = encode(across, down)
        if net:

            @pl.when(n == 1)
            def _():
                gather()

            @pl.when(n > 0)
            def _():
                to_col(lax.rem(own + n, COLS), s1, o, *sems)

        return 0

    lax.fori_loop(0, 8, block, 0)
    if net:
        o[own] = s1[own]
        finish(o, 3, sems[1])
        finish(o, 4, sems[2])
        finish(s1, COLS - 1, sems[0])
    else:
        o[...] = s1[...]


def column_kernel(net, g, d1, tw, f2, m0, o, s1, r1, ure, uim, *sems):
    flat = s1.reshape(1024, 128) if net else s1
    cos, sin = tw[0], tw[1]
    for grp in range(8):
        x, at = [], []
        for i in (2 * grp, 2 * grp + 1):
            x += decode(g[pl.ds(i, 64, stride=16), :])
            at += [i, 16 + i]
        v = dot3(pair(d1), split(jnp.concatenate(x, 1)))
        for j in range(4):
            re = v[:32, j * 128 : (j + 1) * 128]
            im = v[32:, j * 128 : (j + 1) * 128]
            ure[pl.ds(at[j], 32, stride=32), :] = re * cos + im * sin
            uim[pl.ds(at[j], 32, stride=32), :] = im * cos - re * sin
    lane = lax.broadcasted_iota(jnp.int32, (256, 128), 1)

    def send(kg):
        if net and kg >= 0:
            to_col(kg, s1, r1, *sems[:3])
            to_col(kg + 4, s1, r1, *sems[:3])

    for kg in range(4):
        rows = slice(kg * 256, (kg + 1) * 256)
        rhs = split(jnp.concatenate([ure[rows, :], uim[rows, :]], 1))
        out = dot3(pair(f2), rhs, True)
        for h in range(2):
            part = out[:, h * 128 : (h + 1) * 128]
            if kg == 0 and h == 0:
                special = dot3(pair(m0), (rhs[0][:128], rhs[1][:128]), True)
                part = jnp.where(lane < 32, special, part)
            word = encode(part[:128], part[128:])
            for half in range(2):
                at = pl.ds((half * 4 + kg) * 128 + h, 64, stride=2)
                flat[at, :] = word[half * 64 : half * 64 + 64]
        send(kg - 1)
    send(3)
    if net:
        all_exchange(s1, r1, o, sems, True)
    else:
        o[...] = s1[...]


def row_kernel(net, kb, x, e, tw, w2, ka_ref, w3, e4, o, s1, r1, uh, ul, sh, sl, yh, yl, *sems):
    flat = s1.reshape(512, 128) if net else s1
    for c in range(8):
        cos = jnp.concatenate([tw[0, c * 16 : c * 16 + 16, :]] * 8, 0)
        sin = jnp.concatenate([tw[1, c * 16 : c * 16 + 16, :]] * 8, 0)
        for h in range(2):
            block = jnp.concatenate(decode(x[pl.ds(c * 2 + h, 64, stride=16), :]), 0)
            both = dot3(split(block.T), pair(e))
            v, vs = both[:, :128], both[:, 128:]
            u = split(v * cos - vs * sin)
            us = split(vs * cos + v * sin)
            for kf in range(8):
                at = pl.ds((h * 8 + kf) * 128 + c * 16, 16)
                part = slice(kf * 16, kf * 16 + 16)
                uh[at, :] = u[0][part]
                ul[at, :] = u[1][part]
                sh[at, :] = us[0][part]
                sl[at, :] = us[1][part]
    ka = ka_ref[...]
    ka2 = ka * ka + FLOOR * FLOOR
    sign = jnp.where(lax.broadcasted_iota(jnp.int32, (128, 128), 1) < 64, -1.0, 1.0)

    def stack(first, second, col):
        parts = []
        for f in range(2):
            at = slice((col * 2 + f) * 128, (col * 2 + f + 1) * 128)
            parts.append(jnp.concatenate([first[at, :], second[at, :]], 0))
        return jnp.concatenate(parts, 1)

    for pr in range(4):
        q, qs = [], []
        for j in range(2):
            col = pr * 2 + j
            out = dot3(pair(w2), (stack(uh, sh, col), stack(ul, sl, col)))
            wb = kb[col]
            weight = LOCAL_WEIGHT + 1.0 / (ka2 + wb * wb)
            mixed = weight * (wb * out[:, :128] + ka * out[:, 128:])
            q.append(mixed)
            qs.append(pltpu.roll(mixed, 64, 1) * sign)
        rhs = jnp.concatenate([jnp.concatenate(q, 1), jnp.concatenate(qs, 1)], 0)
        back = dot3(pair(w3), split(rhs))
        for j in range(2):
            col = pr * 2 + j
            b = back[:128, j * 128 : (j + 1) * 128]
            bs = back[128:, j * 128 : (j + 1) * 128]
            y = split(b * tw[0] + bs * tw[1])
            for c in range(8):
                at = pl.ds(c * 128 + col * 16, 16)
                yh[at, :] = y[0][c * 16 : c * 16 + 16]
                yl[at, :] = y[1][c * 16 : c * 16 + 16]
    for c in range(8):
        rows = slice(c * 128, (c + 1) * 128)
        out = dot3(pair(e4), (yh[rows, :], yl[rows, :]), True)
        flat[c * 64 : c * 64 + 64, :] = encode(out[:64], out[64:])
        if net and c > 0:
            to_col(c - 1, s1, r1, *sems[:3])
    if net:
        to_col(COLS - 1, s1, r1, *sems[:3])
        all_exchange(s1, r1, o, sems, False)
    else:
        o[...] = s1[...]


def image_kernel(net, t, f4, m0i, tw, d4, o, s1, r1, vre, vim, *sems):

    flat = s1.reshape(512, 128) if net else s1
    for kg in range(4):
        block = decode(t[pl.ds(kg, 128, stride=4), :])
        lhs = split(jnp.concatenate([part.T for part in block], 1))
        v = dot3(lhs, pair(f4))
        if kg == 0:
            special = dot3((lhs[0][:16], lhs[1][:16]), pair(m0i))
            v = jnp.concatenate([special, v[16:]], 0)
        for col in range(8):
            kk = kg * 8 + col
            re = v[col * 16 : col * 16 + 16, :128]
            im = v[col * 16 : col * 16 + 16, 128:]
            cos = tw[0, kk : kk + 1, :]
            sin = tw[1, kk : kk + 1, :]
            vre[kk * 16 : kk * 16 + 16, :] = re * cos - im * sin
            vim[kk * 16 : kk * 16 + 16, :] = im * cos + re * sin
    for grp in range(4):
        picks = (grp * 2, grp * 2 + 8, grp * 2 + 1, grp * 2 + 9)
        cols = []
        for i in picks:
            at = pl.ds(i, 32, stride=16)
            cols.append(jnp.concatenate([vre[at, :], vim[at, :]], 0))
        out = dot3(pair(d4), split(jnp.concatenate(cols, 1)))
        for j in range(2):
            word = encode(out[:, j * 256 : j * 256 + 128], out[:, j * 256 + 128 : j * 256 + 256])
            flat[pl.ds(grp * 2 + j, 64, stride=8), :] = word
    if net:
        own = here()[1]
        for i in range(1, COLS):
            to_col(lax.rem(own + i, COLS), s1, r1, *sems)
        r1[own] = s1[own]
        finish(r1, 3, sems[1])
        finish(r1, 4, sems[2])
    else:
        r1[...] = s1[...]
    for c in range(8):
        halves = decode(r1[c] if net else r1[c * 64 : c * 64 + 64, :])
        for it in range(2):
            for ph in range(8):
                at = slice(c * 16 + it * 8, c * 16 + it * 8 + 8)
                o[at, ph * 128 : ph * 128 + 128] = halves[it][ph * 8 : ph * 8 + 8]
    if net:
        finish(s1, COLS - 1, sems[0])


def whole_kernel(
    kb, x, before, after, slopes, tile, rshift, pshift, frac,
    d1, tw1, f2, m0, e, tw2, w2, ka, w3, e4, f4, m0i, d4, out, *rest,
):
    scratch, sems = rest[:-16], rest[-16:]
    flow_land, s_flow, spec_land, s_spec, r_spec, mix_land, s_mix, r_mix, s_img, r_img = scratch[:10]
    padded, spots, wts, sc, ure, uim, uh, ul, sh, sl, yh, yl, vre, vim = scratch[10:]
    greet()
    pull_kernel(
        True, x, before, after, slopes, tile, rshift, pshift, frac,
        flow_land, s_flow, padded, spots, wts, sc, *sems[:3],
    )
    column_kernel(
        True, flow_land.reshape(1024, 128), d1, tw1, f2, m0,
        spec_land, s_spec, r_spec, ure, uim, *sems[3:8],
    )
    row_kernel(
        True, kb, spec_land.reshape(1024, 128), e, tw2, w2, ka, w3, e4,
        mix_land, s_mix, r_mix, uh, ul, sh, sl, yh, yl, *sems[8:13],
    )
    image_kernel(
        True, mix_land.reshape(512, 128), f4, m0i, tw1, d4,
        out, s_img, r_img, vre, vim, *sems[13:16],
    )


def call(kernel, out, scratch, *args, net=None, phases=1, smem=()):
    specs = [
        pl.BlockSpec(memory_space=pltpu.SMEM if i in smem else pltpu.VMEM)
        for i in range(len(args))
    ]
    params = {}
    if net is not None:
        scratch = scratch + [pltpu.SemaphoreType.DMA] * (2 * phases)
        params["compiler_params"] = pltpu.CompilerParams(collective_id=net, has_side_effects=True)
    return pl.pallas_call(
        functools.partial(kernel, net is not None),
        out_shape=jax.ShapeDtypeStruct(*out),
        in_specs=specs,
        out_specs=pl.BlockSpec(memory_space=pltpu.VMEM),
        scratch_shapes=scratch,
        **params,
    )(*args)


def two(table):
    return jnp.asarray(np.stack(table))


def words(*shape):
    return pltpu.VMEM(shape, jnp.int32)


def pull(x, before, after, slopes, tile, rshift, pshift, frac, net=None):
    flip = lambda y: jnp.transpose(y, (0, 2, 1))
    return call(
        pull_kernel,
        ((8, 128, 128), jnp.int32),
        [
            words(8, 128, 128),
            pltpu.VMEM((2, 144, 1024), F32),
            pltpu.VMEM((16, 128), jnp.int32),
            pltpu.VMEM((6, 16, 128), F32),
            pltpu.VMEM((2, 2, 144, 128), F32),
        ],
        x, before, after, slopes, flip(tile), flip(rshift), flip(pshift), flip(frac),
        net=net,
    )


def column_transform(g, net=None):
    t = tables()
    return call(
        column_kernel,
        ((64, 8, 2, 128) if net is not None else (1024, 128), jnp.int32),
        [words(8, 64, 2, 128) if net is not None else words(1024, 128)] * 2 + [pltpu.VMEM((1024, 128), F32)] * 2,
        g, two(t["d1"]), jnp.asarray(t["tw1"]), two(t["f2"]), two(t["m0"]),
        net=net, phases=2,
    )


def row_transform(x, device, net=None):
    t = tables()
    group, low = device // 4, device % 4
    kk = low * 8 + jnp.arange(8, dtype=jnp.int32)
    b = kk + 64 * group + jnp.where((kk == 0) & (group >= 64), 32, 0)
    kb = jnp.where(b > N // 2, b - N, b).astype(F32) * (2.0 * math.pi / N)
    return call(
        row_kernel,
        ((64, 8, 1, 128) if net is not None else (512, 128), jnp.int32),
        [words(8, 64, 1, 128) if net is not None else words(512, 128)] * 2
        + [pltpu.VMEM((2048, 128), BF16)] * 4
        + [pltpu.VMEM((1024, 128), BF16)] * 2,
        kb, x, two(t["e"]), jnp.asarray(t["tw2"]), two(t["w2"]), jnp.asarray(t["ka"]),
        two(t["w3"]), two(t["e4"]),
        smem=(0,), net=net, phases=2,
    )


def image_transform(y, net=None):
    t = tables()
    return call(
        image_kernel,
        ((128, 1024), F32),
        [words(8, 64, 128) if net is not None else words(512, 128)] * 2 + [pltpu.VMEM((512, 128), F32)] * 2,
        y, two(t["f4"]), two(t["m0i"]), jnp.asarray(t["tw1"]), two(t["d4"]),
        net=net,
    )


def wave_of_columns(device):
    group, low = device // 4, device % 4
    kk = low * 8 + jnp.arange(8, dtype=jnp.int32)
    b = kk + 64 * group + jnp.where((kk == 0) & (group >= 64), 32, 0)
    return jnp.where(b > N // 2, b - N, b).astype(F32) * (2.0 * math.pi / N)


def per_device(residual, field_slopes, source_tile, row_shift, pixel_shift, fraction):
    peers = lax.axis_size("rows")
    up = [(i, i + 1) for i in range(peers - 1)]
    down = [(j, i) for i, j in up]
    before = lax.ppermute(residual[:, -HALO:], "rows", up)
    after = lax.ppermute(residual[:, :HALO], "rows", down)
    device = lax.axis_index("rows") * lax.axis_size("cols") + lax.axis_index("cols")
    flip = lambda y: jnp.transpose(y, (0, 2, 1))
    t = tables()
    plain = lambda name: jnp.asarray(t[name])
    args = (
        wave_of_columns(device), residual, before, after, field_slopes,
        flip(source_tile), flip(row_shift), flip(pixel_shift), flip(fraction),
        two(t["d1"]), plain("tw1"), two(t["f2"]), two(t["m0"]), two(t["e"]), plain("tw2"),
        two(t["w2"]), plain("ka"), two(t["w3"]), two(t["e4"]), two(t["f4"]), two(t["m0i"]),
        two(t["d4"]),
    )
    f32 = lambda *shape: pltpu.VMEM(shape, F32)
    bf16 = lambda *shape: pltpu.VMEM(shape, BF16)
    scratch = (
        [words(8, 128, 128)] * 2
        + [words(64, 8, 2, 128)] + [words(8, 64, 2, 128)] * 2
        + [words(64, 8, 1, 128)] + [words(8, 64, 1, 128)] * 2
        + [words(8, 64, 128)] * 2
        + [f32(2, 144, 1024), words(16, 128), f32(6, 16, 128), f32(2, 2, 144, 128)]
        + [f32(1024, 128)] * 2
        + [bf16(2048, 128)] * 4 + [bf16(1024, 128)] * 2
        + [f32(512, 128)] * 2
        + [pltpu.SemaphoreType.DMA] * 16
    )
    return pl.pallas_call(
        whole_kernel,
        out_shape=jax.ShapeDtypeStruct((128, 1024), F32),
        in_specs=[
            pl.BlockSpec(memory_space=pltpu.VMEM if i else pltpu.SMEM) for i in range(len(args))
        ],
        out_specs=pl.BlockSpec(memory_space=pltpu.VMEM),
        scratch_shapes=scratch,
        compiler_params=pltpu.CompilerParams(collective_id=0, has_side_effects=True),
    )(*args)


def solution(mesh):
    spec = P(None, "rows", "cols")
    return jax.shard_map(
        per_device,
        mesh=mesh,
        in_specs=(spec,) * 6,
        out_specs=P("rows", "cols"),
        check_vma=False,
    )
```

```python
import functools
import math

import jax
import jax.numpy as jnp
import ml_dtypes
import numpy as np
from jax import lax
from jax.experimental import pallas as pl
from jax.experimental.pallas import tpu as pltpu
from jax.sharding import PartitionSpec as P

N = 8192
TILE = 128
HALO = 8
SHIFT = 2
LOCAL_WEIGHT = 0.5
FLOOR = 8.0 * math.pi / N

F32 = jnp.float32
BF16 = jnp.bfloat16
TINY = 1e-18
BIAS = 120.0
STEPS = 16380.0
CENTRE = 16384.0


def split_table(x):
    hi = x.astype(ml_dtypes.bfloat16)
    lo = (x - hi.astype(np.float64)).astype(ml_dtypes.bfloat16)
    return hi, lo


def cs(angle):
    return np.cos(angle), np.sin(angle)


@functools.lru_cache(maxsize=None)
def tables():
    two_pi = 2.0 * np.pi
    t = {}
    p = np.arange(64)[None, :]
    kk = np.arange(32)[:, None]
    c, s = cs(two_pi * ((p * kk) % 64) / 64)
    d1 = np.concatenate([c, -s], 0)
    d1[32] = (-1.0) ** np.arange(64)
    t["d1"] = split_table(d1)
    d4 = np.concatenate([2 * c, -2 * s], 0).T.copy()
    d4[:, 0] = 1.0
    d4[:, 32] = (-1.0) ** np.arange(64)
    t["d4"] = split_table(d4 / (N * N))
    q = np.arange(128)[None, :]
    c, s = cs(two_pi * (kk * q) / N)
    t["tw1"] = np.stack([c, s]).astype(np.float32)
    l = np.arange(128)[:, None]
    c, s = cs(two_pi * ((l * q) % 128) / 128)
    f2 = np.block([[c, s], [-s, c]])
    order = np.concatenate([np.arange(0, 128, 2), np.arange(1, 128, 2)])
    order = np.concatenate([order, 128 + order])
    t["f2"] = split_table(f2[order])
    t["f4"] = split_table(np.block([[c, s], [-s, c]]))
    c32, s32 = cs(two_pi * ((q * (32 + 64 * l)) % N) / N)
    low = l < 64
    alt = np.broadcast_to((-1.0) ** q, (1, 128))
    m0 = np.zeros((256, 256))
    m0[:128, :128] = np.where(low, c, 0.0)
    m0[128:, :128] = np.where(low, -s, 0.0)
    m0[128:129, :128] = alt
    m0[:128, 128:] = np.where(low, 0.0, c32)
    m0[128:, 128:] = np.where(low, 0.0, -s32)
    t["m0"] = split_table(m0[order])
    mi = 2.0 * m0
    mi[0] *= 0.5
    mi[128] *= 0.5
    t["m0i"] = split_table(mi)
    r = np.arange(64)[:, None]
    m = np.arange(64)[None, :]
    c, s = cs(two_pi * ((r * m) % 64) / 64)
    e_re = np.concatenate([c, s], 0)
    e_im = np.concatenate([-s, c], 0)
    t["e"] = split_table(np.concatenate([e_re, e_im, -e_im, e_re], 1))
    t["e4"] = split_table(np.block([[c, -s], [s, c]]))
    q2 = np.arange(128)[:, None]
    mm = np.concatenate([np.arange(64), np.arange(64)])[None, :]
    c, s = cs(two_pi * (q2 * mm) / N)
    t["tw2"] = np.stack([c, s]).astype(np.float32)
    n = np.arange(128)[:, None]
    c, s = cs(two_pi * ((n * q2.T) % 128) / 128)
    t["w2"] = split_table(np.concatenate([c, -s], 1))
    t["w3"] = split_table(np.block([[s, -c], [c, s]]))
    a = mm + 64 * n
    signed = np.where(a > N // 2, a - N, np.where(a == N // 2, 0, a))
    t["ka"] = (signed * (two_pi / N)).astype(np.float32)
    return t


def split(x):
    hi = x.astype(BF16)
    return hi, (x - hi.astype(F32)).astype(BF16)


def dot(a, b, transposed=False):
    dims = (((1,), (1 if transposed else 0,)), ((), ()))
    return lax.dot_general(a, b, dims, preferred_element_type=F32)


def dot3(a, b, transposed=False):
    (ah, al), (bh, bl) = a, b
    return dot(ah, bh, transposed) + (dot(ah, bl, transposed) + dot(al, bh, transposed))


def pair(ref):
    return ref[0], ref[1]


MESH = pl.DeviceIdType.MESH
ROWS, COLS = 64, 8


def here():
    return lax.axis_index("rows"), lax.axis_index("cols")


def greet():
    r, c = here()
    barrier = pltpu.get_barrier_semaphore()
    for i in range(1, COLS):
        peer = (r, lax.rem(c + i, COLS))
        pl.semaphore_signal(barrier, inc=1, device_id=peer, device_id_type=MESH)

    def signal(i, _):
        peer = (lax.rem(r + i, ROWS), c)
        pl.semaphore_signal(barrier, inc=1, device_id=peer, device_id_type=MESH)
        return 0

    lax.fori_loop(1, ROWS, signal, 0)


def gather():
    pl.semaphore_wait(pltpu.get_barrier_semaphore(), COLS - 1 + ROWS - 1)


def remote(src, dst, sems, peer):
    pltpu.make_async_remote_copy(
        src_ref=src,
        dst_ref=dst,
        send_sem=sems[0],
        recv_sem=sems[1],
        device_id=peer,
        device_id_type=MESH,
    ).start()


def to_col(peer, src, dst, send, near, far):
    r, c = here()
    same = lax.div(c, 4) == peer // 4 if isinstance(peer, int) else lax.div(c, 4) == lax.div(peer, 4)

    @pl.when(same & (peer != c))
    def _():
        remote(src.at[peer], dst.at[c], (send, near), (r, peer))

    @pl.when(jnp.logical_not(same))
    def _():
        remote(src.at[peer], dst.at[c], (send, far), (r, peer))


def finish(ref, count, sem):
    part = ref.at[pl.ds(0, count)]
    pltpu.make_async_copy(part, part, sem).wait()


def to_rows(src, dst, sems, first, count):
    r, c = here()

    def send(i, _):
        peer = lax.rem(r + lax.rem(i * 27, ROWS), ROWS)
        remote(
            src.at[pl.ds(first, count), peer], dst.at[r, pl.ds(first, count)], sems, (peer, c)
        )
        return 0

    lax.fori_loop(1, ROWS, send, 0)


def all_exchange(s1, r1, o, sems, split_groups):
    send1, near, far, send2, recv2 = sems
    r, c = here()
    r1[c] = s1[c]
    own = lax.div(c, 4) * 4
    finish(r1, 3, near)
    if split_groups:
        to_rows(r1, o, (send2, recv2), own, 4)
        finish(r1, 4, far)
        to_rows(r1, o, (send2, recv2), 4 - own, 4)
    else:
        finish(r1, 4, far)
        to_rows(r1, o, (send2, recv2), 0, 8)
    o[r] = r1[:, r]
    finish(o, ROWS - 1, recv2)
    finish(s1, COLS - 1, send1)
    finish(o, ROWS - 1, send2)


def spread(x, join):
    x = join(x, pltpu.roll(x, 64, 1))
    return join(x, pltpu.roll(x, 32, 1))


def lane_field(shape):
    return lax.shift_left(
        lax.shift_right_logical(lax.broadcasted_iota(jnp.int32, shape, 1), 5), 1
    )


def encode(x, y):
    peak = spread(jnp.maximum(jnp.abs(x), jnp.abs(y)), jnp.maximum)
    level = jnp.ceil(2.0 * jnp.log2(jnp.maximum(peak, TINY))) + BIAS
    level = jnp.clip(level, 0.0, 255.0)
    gain = jnp.exp2((BIAS - level) * 0.5) * STEPS
    code = level.astype(jnp.int32)
    bits = lax.shift_right_logical(code, lane_field(x.shape)) & 3
    qx = (x * gain + (CENTRE + 0.5)).astype(jnp.int32)
    qy = (y * gain + (CENTRE + 0.5)).astype(jnp.int32)
    return qx | lax.shift_left(qy, 15) | lax.shift_left(bits, 30)


def decode(word):
    bits = lax.shift_right_logical(word, 30) & 3
    code = spread(lax.shift_left(bits, lane_field(word.shape)), jnp.add)
    scale = jnp.exp2((code.astype(F32) - BIAS) * 0.5) * (1.0 / STEPS)
    x = (word & 32767).astype(F32) - CENTRE
    y = (lax.shift_right_logical(word, 15) & 32767).astype(F32) - CENTRE
    return x * scale, y * scale


def pull_kernel(
    net, x, before, after, slopes, tile, rshift, pshift, frac, o, s1, padded, spots, wts, sc,
    *link,
):
    own = here()[1] if net else 0
    if net:
        stage, land, *sems = link
        stage[0] = x[:, 128 - HALO :, :]
        stage[1] = x[:, :HALO, :]
    padded[:, HALO : HALO + 128, :] = x[...].astype(F32)
    sc[:, :, 0:8, :] = jnp.zeros((2, 2, 8, 128), F32)
    sc[:, :, 136:144, :] = jnp.zeros((2, 2, 8, 128), F32)
    lane = lax.broadcasted_iota(jnp.int32, (8, 128), 1)

    def by_block(values):
        out = jnp.zeros((8, 128), values.dtype)
        for t in range(8):
            row = jnp.broadcast_to(values[t : t + 1, :], (8, 128))
            row = pltpu.roll(pltpu.roll(row, (16 * t + 16) % 128, 1), 0, 1, stride=16, stride_axis=0)
            out = jnp.where((lane >= 16 * t) & (lane < 16 * t + 16), row, out)
        return out

    for k in range(2):
        rows = slice(k * 8, k * 8 + 8)
        index = tile[k] * 32 + (lax.rem(lane, 16) + HALO) + rshift[k]
        spots[rows, :] = by_block(index)
        ps = by_block(pshift[k])
        f = by_block(frac[k])
        for oi in range(6):
            off = oi - SHIFT
            wts[oi, rows, :] = jnp.where(ps == off, 1.0 - f, 0.0) + jnp.where(
                ps + 1 == off, f, 0.0
            )
    place = lax.broadcasted_iota(jnp.int32, (256, 128), 0)

    def block(b):
        r0 = pl.multiple_of(b * 16, 16)
        window = [
            jnp.concatenate(
                [padded[p, pl.ds(r0, 32), u * 128 : (u + 1) * 128] for u in range(8)], 0
            )
            for p in range(2)
        ]
        window = jnp.concatenate(window, 1).astype(BF16)
        hot = jnp.concatenate(
            [
                jnp.where(place == spots[pl.ds(k * 8 + 7 - b, 1), :], 1.0, 0.0).astype(BF16)
                for k in range(2)
            ],
            1,
        )
        picked = lax.dot_general(
            window, hot, (((0,), (0,)), ((), ())), preferred_element_type=F32
        )
        for p in range(2):
            for k in range(2):
                sc[p, k, 8:136, :] = picked[p * 128 : p * 128 + 128, k * 128 : k * 128 + 128]
        got = []
        for p in range(2):
            total = None
            for oi in range(6):
                for k in range(2):
                    w = wts[oi, pl.ds(k * 8 + 7 - b, 1), :]
                    part = w * sc[p, k, 8 + oi - SHIFT : 136 + oi - SHIFT, :]
                    total = part if total is None else total + part
            got.append(total.T)
        for t in range(8):
            at = slice(t * 16, t * 16 + 16)
            first, second = got[0][at], got[1][at]
            s = [slopes[i, pl.ds(r0, 16), t * 128 : (t + 1) * 128].astype(F32) for i in range(4)]
            across = -(first * s[0] + second * s[1])
            down = -(first * s[2] + second * s[3])
            s1[b, t * 16 : t * 16 + 16, :] = encode(across, down)

    def inner(n, _):
        block(1 + lax.rem(own + n, 6))
        return 0

    def edge(n, _):
        block(7 * lax.rem(own + n, 2))
        return 0

    lax.fori_loop(0, 6, inner, 0)
    if net:
        r, c = here()
        gather()
        remote(stage.at[0], land.at[0], (sems[3], sems[4]), (lax.rem(r + 1, ROWS), c))
        remote(stage.at[1], land.at[1], (sems[3], sems[5]), (lax.rem(r + ROWS - 1, ROWS), c))
        for i in range(1, COLS):
            peer = lax.rem(own + i, COLS)

            @pl.when((peer > 0) & (peer < COLS - 1))
            def _():
                to_col(peer, s1, o, *sems[:3])

        finish(land, 1, sems[4])
        finish(land, 1, sems[5])
        padded[:, 0:HALO, :] = jnp.where(r > 0, land[0].astype(F32), 0.0)
        padded[:, HALO + 128 :, :] = jnp.where(r < ROWS - 1, land[1].astype(F32), 0.0)
    else:
        padded[:, 0:HALO, :] = before[...].astype(F32)
        padded[:, HALO + 128 :, :] = after[...].astype(F32)
    lax.fori_loop(0, 2, edge, 0)
    if net:
        o[own] = s1[own]
        to_col(0, s1, o, *sems[:3])
        to_col(COLS - 1, s1, o, *sems[:3])
        finish(o, 3, sems[1])
        finish(o, 4, sems[2])
        finish(s1, COLS - 1, sems[0])
        finish(stage, 2, sems[3])
    else:
        o[...] = s1[...]


def column_kernel(net, g, d1, tw, f2, m0, o, s1, r1, ure, uim, *sems):
    flat = s1.reshape(1024, 128) if net else s1
    cos, sin = tw[0], tw[1]
    for grp in range(8):
        x, at = [], []
        for i in (2 * grp, 2 * grp + 1):
            x += decode(g[pl.ds(i, 64, stride=16), :])
            at += [i, 16 + i]
        v = dot3(pair(d1), split(jnp.concatenate(x, 1)))
        for j in range(4):
            re = v[:32, j * 128 : (j + 1) * 128]
            im = v[32:, j * 128 : (j + 1) * 128]
            ure[pl.ds(at[j], 32, stride=32), :] = re * cos + im * sin
            uim[pl.ds(at[j], 32, stride=32), :] = im * cos - re * sin
    lane = lax.broadcasted_iota(jnp.int32, (256, 128), 1)

    def send(kg):
        if net and kg >= 0:
            to_col(kg, s1, r1, *sems[:3])
            to_col(kg + 4, s1, r1, *sems[:3])

    for kg in range(4):
        rows = slice(kg * 256, (kg + 1) * 256)
        rhs = split(jnp.concatenate([ure[rows, :], uim[rows, :]], 1))
        out = dot3(pair(f2), rhs, True)
        for h in range(2):
            part = out[:, h * 128 : (h + 1) * 128]
            if kg == 0 and h == 0:
                special = dot3(pair(m0), (rhs[0][:128], rhs[1][:128]), True)
                part = jnp.where(lane < 32, special, part)
            word = encode(part[:128], part[128:])
            for half in range(2):
                at = pl.ds((half * 4 + kg) * 128 + h, 64, stride=2)
                flat[at, :] = word[half * 64 : half * 64 + 64]
        send(kg - 1)
    send(3)
    if net:
        all_exchange(s1, r1, o, sems, True)
    else:
        o[...] = s1[...]


def column_wave(col):
    r, c = here()
    group = r * 2 + lax.div(c, 4)
    b = lax.rem(c, 4) * 8 + col + 64 * group
    if col == 0:
        b = b + jnp.where((lax.rem(c, 4) == 0) & (group >= 64), 32, 0)
    return jnp.where(b > N // 2, b - N, b).astype(F32) * (2.0 * math.pi / N)


def row_kernel(net, kb, x, e, tw, w2, ka_ref, w3, e4, o, s1, r1, uh, ul, sh, sl, yh, yl, *sems):
    flat = s1.reshape(512, 128) if net else s1
    for c in range(8):
        cos = jnp.concatenate([tw[0, c * 16 : c * 16 + 16, :]] * 8, 0)
        sin = jnp.concatenate([tw[1, c * 16 : c * 16 + 16, :]] * 8, 0)
        for h in range(2):
            block = jnp.concatenate(decode(x[pl.ds(c * 2 + h, 64, stride=16), :]), 0)
            both = dot3(split(block.T), pair(e))
            v, vs = both[:, :128], both[:, 128:]
            u = split(v * cos - vs * sin)
            us = split(vs * cos + v * sin)
            for kf in range(8):
                at = pl.ds((h * 8 + kf) * 128 + c * 16, 16)
                part = slice(kf * 16, kf * 16 + 16)
                uh[at, :] = u[0][part]
                ul[at, :] = u[1][part]
                sh[at, :] = us[0][part]
                sl[at, :] = us[1][part]
    ka = ka_ref[...]
    ka2 = ka * ka + FLOOR * FLOOR
    sign = jnp.where(lax.broadcasted_iota(jnp.int32, (128, 128), 1) < 64, -1.0, 1.0)

    def stack(first, second, col):
        parts = []
        for f in range(2):
            at = slice((col * 2 + f) * 128, (col * 2 + f + 1) * 128)
            parts.append(jnp.concatenate([first[at, :], second[at, :]], 0))
        return jnp.concatenate(parts, 1)

    for pr in range(4):
        q, qs = [], []
        for j in range(2):
            col = pr * 2 + j
            out = dot3(pair(w2), (stack(uh, sh, col), stack(ul, sl, col)))
            wb = column_wave(col) if net else kb[col]
            weight = LOCAL_WEIGHT + 1.0 / (ka2 + wb * wb)
            mixed = weight * (wb * out[:, :128] + ka * out[:, 128:])
            q.append(mixed)
            qs.append(pltpu.roll(mixed, 64, 1) * sign)
        rhs = jnp.concatenate([jnp.concatenate(q, 1), jnp.concatenate(qs, 1)], 0)
        back = dot3(pair(w3), split(rhs))
        for j in range(2):
            col = pr * 2 + j
            b = back[:128, j * 128 : (j + 1) * 128]
            bs = back[128:, j * 128 : (j + 1) * 128]
            y = split(b * tw[0] + bs * tw[1])
            for c in range(8):
                at = pl.ds(c * 128 + col * 16, 16)
                yh[at, :] = y[0][c * 16 : c * 16 + 16]
                yl[at, :] = y[1][c * 16 : c * 16 + 16]
    for c in range(8):
        rows = slice(c * 128, (c + 1) * 128)
        out = dot3(pair(e4), (yh[rows, :], yl[rows, :]), True)
        flat[c * 64 : c * 64 + 64, :] = encode(out[:64], out[64:])
        if net and c > 0:
            to_col(c - 1, s1, r1, *sems[:3])
    if net:
        to_col(COLS - 1, s1, r1, *sems[:3])
        all_exchange(s1, r1, o, sems, False)
    else:
        o[...] = s1[...]


def image_kernel(net, t, f4, m0i, tw, d4, o, s1, r1, vre, vim, *sems):

    flat = s1.reshape(512, 128) if net else s1
    for kg in range(4):
        block = decode(t[pl.ds(kg, 128, stride=4), :])
        lhs = split(jnp.concatenate([part.T for part in block], 1))
        v = dot3(lhs, pair(f4))
        if kg == 0:
            special = dot3((lhs[0][:16], lhs[1][:16]), pair(m0i))
            v = jnp.concatenate([special, v[16:]], 0)
        for col in range(8):
            kk = kg * 8 + col
            re = v[col * 16 : col * 16 + 16, :128]
            im = v[col * 16 : col * 16 + 16, 128:]
            cos = tw[0, kk : kk + 1, :]
            sin = tw[1, kk : kk + 1, :]
            vre[kk * 16 : kk * 16 + 16, :] = re * cos - im * sin
            vim[kk * 16 : kk * 16 + 16, :] = im * cos + re * sin
    for grp in range(4):
        picks = (grp * 2, grp * 2 + 8, grp * 2 + 1, grp * 2 + 9)
        cols = []
        for i in picks:
            at = pl.ds(i, 32, stride=16)
            cols.append(jnp.concatenate([vre[at, :], vim[at, :]], 0))
        out = dot3(pair(d4), split(jnp.concatenate(cols, 1)))
        for j in range(2):
            word = encode(out[:, j * 256 : j * 256 + 128], out[:, j * 256 + 128 : j * 256 + 256])
            flat[pl.ds(grp * 2 + j, 64, stride=8), :] = word
    if net:
        own = here()[1]
        for i in range(1, COLS):
            to_col(lax.rem(own + i, COLS), s1, r1, *sems)
        r1[own] = s1[own]
        finish(r1, 3, sems[1])
        finish(r1, 4, sems[2])
    else:
        r1[...] = s1[...]
    for c in range(8):
        halves = decode(r1[c] if net else r1[c * 64 : c * 64 + 64, :])
        for it in range(2):
            for ph in range(8):
                at = slice(c * 16 + it * 8, c * 16 + it * 8 + 8)
                o[at, ph * 128 : ph * 128 + 128] = halves[it][ph * 8 : ph * 8 + 8]
    if net:
        finish(s1, COLS - 1, sems[0])


def whole_kernel(
    x, slopes, tile, rshift, pshift, frac,
    d1, tw1, f2, m0, e, tw2, w2, ka, w3, e4, f4, m0i, d4, out, *rest,
):
    scratch, sems = rest[:-19], rest[-19:]
    flow_land, s_flow, spec_land, s_spec, r_spec, mix_land, s_mix, r_mix, s_img, r_img = scratch[:10]
    padded, spots, wts, sc, ure, uim, uh, ul, sh, sl, yh, yl, vre, vim, stage, land = scratch[10:]
    greet()
    pull_kernel(
        True, x, None, None, slopes, tile, rshift, pshift, frac,
        flow_land, s_flow, padded, spots, wts, sc, stage, land, *sems[:3], *sems[16:],
    )
    column_kernel(
        True, flow_land.reshape(1024, 128), d1, tw1, f2, m0,
        spec_land, s_spec, r_spec, ure, uim, *sems[3:8],
    )
    row_kernel(
        True, None, spec_land.reshape(1024, 128), e, tw2, w2, ka, w3, e4,
        mix_land, s_mix, r_mix, uh, ul, sh, sl, yh, yl, *sems[8:13],
    )
    image_kernel(
        True, mix_land.reshape(512, 128), f4, m0i, tw1, d4,
        out, s_img, r_img, vre, vim, *sems[13:16],
    )


def call(kernel, out, scratch, *args, net=None, phases=1, smem=()):
    specs = [
        pl.BlockSpec(memory_space=pltpu.SMEM if i in smem else pltpu.VMEM)
        for i in range(len(args))
    ]
    params = {}
    if net is not None:
        scratch = scratch + [pltpu.SemaphoreType.DMA] * (2 * phases)
        params["compiler_params"] = pltpu.CompilerParams(collective_id=net, has_side_effects=True)
    return pl.pallas_call(
        functools.partial(kernel, net is not None),
        out_shape=jax.ShapeDtypeStruct(*out),
        in_specs=specs,
        out_specs=pl.BlockSpec(memory_space=pltpu.VMEM),
        scratch_shapes=scratch,
        **params,
    )(*args)


def two(table):
    return jnp.asarray(np.stack(table))


def words(*shape):
    return pltpu.VMEM(shape, jnp.int32)


def pull(x, before, after, slopes, tile, rshift, pshift, frac, net=None):
    flip = lambda y: jnp.transpose(y, (0, 2, 1))
    return call(
        pull_kernel,
        ((8, 128, 128), jnp.int32),
        [
            words(8, 128, 128),
            pltpu.VMEM((2, 144, 1024), F32),
            pltpu.VMEM((16, 128), jnp.int32),
            pltpu.VMEM((6, 16, 128), F32),
            pltpu.VMEM((2, 2, 144, 128), F32),
        ],
        x, before, after, slopes, flip(tile), flip(rshift), flip(pshift), flip(frac),
        net=net,
    )


def column_transform(g, net=None):
    t = tables()
    return call(
        column_kernel,
        ((64, 8, 2, 128) if net is not None else (1024, 128), jnp.int32),
        [words(8, 64, 2, 128) if net is not None else words(1024, 128)] * 2 + [pltpu.VMEM((1024, 128), F32)] * 2,
        g, two(t["d1"]), jnp.asarray(t["tw1"]), two(t["f2"]), two(t["m0"]),
        net=net, phases=2,
    )


def row_transform(x, device, net=None):
    t = tables()
    group, low = device // 4, device % 4
    kk = low * 8 + jnp.arange(8, dtype=jnp.int32)
    b = kk + 64 * group + jnp.where((kk == 0) & (group >= 64), 32, 0)
    kb = jnp.where(b > N // 2, b - N, b).astype(F32) * (2.0 * math.pi / N)
    return call(
        row_kernel,
        ((64, 8, 1, 128) if net is not None else (512, 128), jnp.int32),
        [words(8, 64, 1, 128) if net is not None else words(512, 128)] * 2
        + [pltpu.VMEM((2048, 128), BF16)] * 4
        + [pltpu.VMEM((1024, 128), BF16)] * 2,
        kb, x, two(t["e"]), jnp.asarray(t["tw2"]), two(t["w2"]), jnp.asarray(t["ka"]),
        two(t["w3"]), two(t["e4"]),
        smem=(0,), net=net, phases=2,
    )


def image_transform(y, net=None):
    t = tables()
    return call(
        image_kernel,
        ((128, 1024), F32),
        [words(8, 64, 128) if net is not None else words(512, 128)] * 2 + [pltpu.VMEM((512, 128), F32)] * 2,
        y, two(t["f4"]), two(t["m0i"]), jnp.asarray(t["tw1"]), two(t["d4"]),
        net=net,
    )


def per_device(residual, field_slopes, source_tile, row_shift, pixel_shift, fraction):
    flip = lambda y: jnp.transpose(y, (0, 2, 1))
    t = tables()
    plain = lambda name: jnp.asarray(t[name])
    args = (
        residual, field_slopes,
        flip(source_tile), flip(row_shift), flip(pixel_shift), flip(fraction),
        two(t["d1"]), plain("tw1"), two(t["f2"]), two(t["m0"]), two(t["e"]), plain("tw2"),
        two(t["w2"]), plain("ka"), two(t["w3"]), two(t["e4"]), two(t["f4"]), two(t["m0i"]),
        two(t["d4"]),
    )
    f32 = lambda *shape: pltpu.VMEM(shape, F32)
    bf16 = lambda *shape: pltpu.VMEM(shape, BF16)
    scratch = (
        [words(8, 128, 128)] * 2
        + [words(64, 8, 2, 128)] + [words(8, 64, 2, 128)] * 2
        + [words(64, 8, 1, 128)] + [words(8, 64, 1, 128)] * 2
        + [words(8, 64, 128)] * 2
        + [f32(2, 144, 1024), words(16, 128), f32(6, 16, 128), f32(2, 2, 144, 128)]
        + [f32(1024, 128)] * 2
        + [bf16(2048, 128)] * 4 + [bf16(1024, 128)] * 2
        + [f32(512, 128)] * 2
        + [bf16(2, 2, 8, 1024)] * 2
        + [pltpu.SemaphoreType.DMA] * 19
    )
    return pl.pallas_call(
        whole_kernel,
        out_shape=pltpu.VMEM((128, 1024), F32),
        in_specs=[pl.BlockSpec(memory_space=pltpu.VMEM)] * len(args),
        out_specs=pl.BlockSpec(memory_space=pltpu.VMEM),
        scratch_shapes=scratch,
        compiler_params=pltpu.CompilerParams(collective_id=0, has_side_effects=True),
    )(*args)


def solution(mesh):
    spec = P(None, "rows", "cols")
    return jax.shard_map(
        per_device,
        mesh=mesh,
        in_specs=(spec,) * 6,
        out_specs=P("rows", "cols"),
        check_vma=False,
    )
```

```python
import functools
import math

import jax
import jax.numpy as jnp
import ml_dtypes
import numpy as np
from jax import lax
from jax.experimental import pallas as pl
from jax.experimental.pallas import tpu as pltpu
from jax.sharding import PartitionSpec as P

N = 8192
TILE = 128
HALO = 8
SHIFT = 2
LOCAL_WEIGHT = 0.5
FLOOR = 8.0 * math.pi / N

F32 = jnp.float32
BF16 = jnp.bfloat16
TINY = 1e-18
BIAS = 120.0
STEPS = 16380.0
CENTRE = 16384.0


def split_table(x):
    hi = x.astype(ml_dtypes.bfloat16)
    lo = (x - hi.astype(np.float64)).astype(ml_dtypes.bfloat16)
    return hi, lo


def cs(angle):
    return np.cos(angle), np.sin(angle)


@functools.lru_cache(maxsize=None)
def tables():
    two_pi = 2.0 * np.pi
    t = {}
    p = np.arange(64)[None, :]
    kk = np.arange(32)[:, None]
    c, s = cs(two_pi * ((p * kk) % 64) / 64)
    d1 = np.concatenate([c, -s], 0)
    d1[32] = (-1.0) ** np.arange(64)
    t["d1"] = split_table(d1)
    d4 = np.concatenate([2 * c, -2 * s], 0).T.copy()
    d4[:, 0] = 1.0
    d4[:, 32] = (-1.0) ** np.arange(64)
    t["d4"] = split_table(d4 / (N * N))
    q = np.arange(128)[None, :]
    c, s = cs(two_pi * (kk * q) / N)
    t["tw1"] = np.stack([c, s]).astype(np.float32)
    l = np.arange(128)[:, None]
    c, s = cs(two_pi * ((l * q) % 128) / 128)
    f2 = np.block([[c, s], [-s, c]])
    order = np.concatenate([np.arange(0, 128, 2), np.arange(1, 128, 2)])
    order = np.concatenate([order, 128 + order])
    t["f2"] = split_table(f2[order])
    t["f4"] = split_table(np.block([[c, s], [-s, c]]))
    c32, s32 = cs(two_pi * ((q * (32 + 64 * l)) % N) / N)
    low = l < 64
    alt = np.broadcast_to((-1.0) ** q, (1, 128))
    m0 = np.zeros((256, 256))
    m0[:128, :128] = np.where(low, c, 0.0)
    m0[128:, :128] = np.where(low, -s, 0.0)
    m0[128:129, :128] = alt
    m0[:128, 128:] = np.where(low, 0.0, c32)
    m0[128:, 128:] = np.where(low, 0.0, -s32)
    t["m0"] = split_table(m0[order])
    mi = 2.0 * m0
    mi[0] *= 0.5
    mi[128] *= 0.5
    t["m0i"] = split_table(mi)
    r = np.arange(64)[:, None]
    m = np.arange(64)[None, :]
    c, s = cs(two_pi * ((r * m) % 64) / 64)
    e_re = np.concatenate([c, s], 0)
    e_im = np.concatenate([-s, c], 0)
    t["e"] = split_table(np.concatenate([e_re, e_im, -e_im, e_re], 1))
    t["e4"] = split_table(np.block([[c, -s], [s, c]]))
    q2 = np.arange(128)[:, None]
    mm = np.concatenate([np.arange(64), np.arange(64)])[None, :]
    c, s = cs(two_pi * (q2 * mm) / N)
    t["tw2"] = np.stack([c, s]).astype(np.float32)
    n = np.arange(128)[:, None]
    c, s = cs(two_pi * ((n * q2.T) % 128) / 128)
    t["w2"] = split_table(np.concatenate([c, -s], 1))
    t["w3"] = split_table(np.block([[s, -c], [c, s]]))
    a = mm + 64 * n
    signed = np.where(a > N // 2, a - N, np.where(a == N // 2, 0, a))
    t["ka"] = (signed * (two_pi / N)).astype(np.float32)
    return t


def split(x):
    hi = x.astype(BF16)
    return hi, (x - hi.astype(F32)).astype(BF16)


def dot(a, b, transposed=False):
    dims = (((1,), (1 if transposed else 0,)), ((), ()))
    return lax.dot_general(a, b, dims, preferred_element_type=F32)


def dot3(a, b, transposed=False):
    (ah, al), (bh, bl) = a, b
    return dot(ah, bh, transposed) + (dot(ah, bl, transposed) + dot(al, bh, transposed))


def pair(ref):
    return ref[0], ref[1]


MESH = pl.DeviceIdType.MESH
ROWS, COLS = 64, 8


def here():
    return lax.axis_index("rows"), lax.axis_index("cols")


def greet():
    r, c = here()
    barrier = pltpu.get_barrier_semaphore()
    for i in range(1, COLS):
        peer = (r, lax.rem(c + i, COLS))
        pl.semaphore_signal(barrier, inc=1, device_id=peer, device_id_type=MESH)

    def signal(i, _):
        peer = (lax.rem(r + i, ROWS), c)
        pl.semaphore_signal(barrier, inc=1, device_id=peer, device_id_type=MESH)
        return 0

    lax.fori_loop(1, ROWS, signal, 0)


def gather():
    pl.semaphore_wait(pltpu.get_barrier_semaphore(), COLS - 1 + ROWS - 1)


def remote(src, dst, sems, peer):
    pltpu.make_async_remote_copy(
        src_ref=src,
        dst_ref=dst,
        send_sem=sems[0],
        recv_sem=sems[1],
        device_id=peer,
        device_id_type=MESH,
    ).start()


def to_col(peer, src, dst, send, near, far):
    r, c = here()
    same = lax.div(c, 4) == peer // 4 if isinstance(peer, int) else lax.div(c, 4) == lax.div(peer, 4)

    @pl.when(same & (peer != c))
    def _():
        remote(src.at[peer], dst.at[c], (send, near), (r, peer))

    @pl.when(jnp.logical_not(same))
    def _():
        remote(src.at[peer], dst.at[c], (send, far), (r, peer))


def finish(ref, count, sem):
    part = ref.at[pl.ds(0, count)]
    pltpu.make_async_copy(part, part, sem).wait()


def to_rows(src, dst, sems, first, count):
    r, c = here()

    def send(i, _):
        peer = lax.rem(r + lax.rem(i * 27, ROWS), ROWS)
        remote(
            src.at[pl.ds(first, count), peer], dst.at[r, pl.ds(first, count)], sems, (peer, c)
        )
        return 0

    lax.fori_loop(1, ROWS, send, 0)


def all_exchange(s1, r1, o, sems, split_groups):
    send1, near, far, send2, recv2 = sems
    r, c = here()
    r1[c] = s1[c]
    own = lax.div(c, 4) * 4
    finish(r1, 3, near)
    if split_groups:
        to_rows(r1, o, (send2, recv2), own, 4)
        finish(r1, 4, far)
        to_rows(r1, o, (send2, recv2), 4 - own, 4)
    else:
        finish(r1, 4, far)
        to_rows(r1, o, (send2, recv2), 0, 8)
    o[r] = r1[:, r]
    finish(o, ROWS - 1, recv2)
    finish(s1, COLS - 1, send1)
    finish(o, ROWS - 1, send2)


def spread(x, join):
    x = join(x, pltpu.roll(x, 64, 1))
    return join(x, pltpu.roll(x, 32, 1))


def lane_field(shape):
    return lax.shift_left(
        lax.shift_right_logical(lax.broadcasted_iota(jnp.int32, shape, 1), 5), 1
    )


def encode(x, y):
    peak = spread(jnp.maximum(jnp.abs(x), jnp.abs(y)), jnp.maximum)
    level = jnp.ceil(2.0 * jnp.log2(jnp.maximum(peak, TINY))) + BIAS
    level = jnp.clip(level, 0.0, 255.0)
    gain = jnp.exp2((BIAS - level) * 0.5) * STEPS
    code = level.astype(jnp.int32)
    bits = lax.shift_right_logical(code, lane_field(x.shape)) & 3
    qx = (x * gain + (CENTRE + 0.5)).astype(jnp.int32)
    qy = (y * gain + (CENTRE + 0.5)).astype(jnp.int32)
    return qx | lax.shift_left(qy, 15) | lax.shift_left(bits, 30)


def decode(word):
    bits = lax.shift_right_logical(word, 30) & 3
    code = spread(lax.shift_left(bits, lane_field(word.shape)), jnp.add)
    scale = jnp.exp2((code.astype(F32) - BIAS) * 0.5) * (1.0 / STEPS)
    x = (word & 32767).astype(F32) - CENTRE
    y = (lax.shift_right_logical(word, 15) & 32767).astype(F32) - CENTRE
    return x * scale, y * scale


def pull_kernel(
    net, x, before, after, slopes, tile, rshift, pshift, frac, o, s1, padded, spots, wts, sc,
    *link,
):
    own = here()[1] if net else 0
    if net:
        stage, land, *sems = link
        stage[0] = x[:, 128 - HALO :, :]
        stage[1] = x[:, :HALO, :]
    padded[:, HALO : HALO + 128, :] = x[...].astype(F32)
    sc[:, :, 0:8, :] = jnp.zeros((2, 2, 8, 128), F32)
    sc[:, :, 136:144, :] = jnp.zeros((2, 2, 8, 128), F32)
    lane = lax.broadcasted_iota(jnp.int32, (8, 128), 1)

    def by_block(values):
        out = jnp.zeros((8, 128), values.dtype)
        for t in range(8):
            row = jnp.broadcast_to(values[t : t + 1, :], (8, 128))
            row = pltpu.roll(pltpu.roll(row, (16 * t + 16) % 128, 1), 0, 1, stride=16, stride_axis=0)
            out = jnp.where((lane >= 16 * t) & (lane < 16 * t + 16), row, out)
        return out

    for k in range(2):
        rows = slice(k * 8, k * 8 + 8)
        index = tile[k] * 32 + (lax.rem(lane, 16) + HALO) + rshift[k]
        spots[rows, :] = by_block(index)
        ps = by_block(pshift[k])
        f = by_block(frac[k])
        for oi in range(6):
            off = oi - SHIFT
            wts[oi, rows, :] = jnp.where(ps == off, 1.0 - f, 0.0) + jnp.where(
                ps + 1 == off, f, 0.0
            )
    place = lax.broadcasted_iota(jnp.int32, (256, 128), 0)

    def block(b):
        r0 = pl.multiple_of(b * 16, 16)
        window = [
            jnp.concatenate(
                [padded[p, pl.ds(r0, 32), u * 128 : (u + 1) * 128] for u in range(8)], 0
            )
            for p in range(2)
        ]
        window = jnp.concatenate(window, 1).astype(BF16)
        hot = jnp.concatenate(
            [
                jnp.where(place == spots[pl.ds(k * 8 + 7 - b, 1), :], 1.0, 0.0).astype(BF16)
                for k in range(2)
            ],
            1,
        )
        picked = lax.dot_general(
            window, hot, (((0,), (0,)), ((), ())), preferred_element_type=F32
        )
        for p in range(2):
            for k in range(2):
                sc[p, k, 8:136, :] = picked[p * 128 : p * 128 + 128, k * 128 : k * 128 + 128]
        got = []
        for p in range(2):
            total = None
            for oi in range(6):
                for k in range(2):
                    w = wts[oi, pl.ds(k * 8 + 7 - b, 1), :]
                    part = w * sc[p, k, 8 + oi - SHIFT : 136 + oi - SHIFT, :]
                    total = part if total is None else total + part
            got.append(total.T)
        for t in range(8):
            at = slice(t * 16, t * 16 + 16)
            first, second = got[0][at], got[1][at]
            s = [slopes[i, pl.ds(r0, 16), t * 128 : (t + 1) * 128].astype(F32) for i in range(4)]
            across = -(first * s[0] + second * s[1])
            down = -(first * s[2] + second * s[3])
            s1[b, t * 16 : t * 16 + 16, :] = encode(across, down)

    def inner(n, _):
        block(1 + lax.rem(own + n, 6))
        return 0

    def edge(n, _):
        block(7 * lax.rem(own + n, 2))
        return 0

    lax.fori_loop(0, 6, inner, 0)
    if net:
        r, c = here()
        gather()
        remote(stage.at[0], land.at[0], (sems[3], sems[4]), (lax.rem(r + 1, ROWS), c))
        remote(stage.at[1], land.at[1], (sems[3], sems[5]), (lax.rem(r + ROWS - 1, ROWS), c))
        for i in range(1, COLS):
            peer = lax.rem(own + i, COLS)

            @pl.when((peer > 0) & (peer < COLS - 1))
            def _():
                to_col(peer, s1, o, *sems[:3])

        finish(land, 1, sems[4])
        finish(land, 1, sems[5])
        padded[:, 0:HALO, :] = jnp.where(r > 0, land[0].astype(F32), 0.0)
        padded[:, HALO + 128 :, :] = jnp.where(r < ROWS - 1, land[1].astype(F32), 0.0)
    else:
        padded[:, 0:HALO, :] = before[...].astype(F32)
        padded[:, HALO + 128 :, :] = after[...].astype(F32)
    lax.fori_loop(0, 2, edge, 0)
    if net:
        o[own] = s1[own]
        to_col(0, s1, o, *sems[:3])
        to_col(COLS - 1, s1, o, *sems[:3])
        finish(o, 3, sems[1])
        finish(o, 4, sems[2])
        finish(s1, COLS - 1, sems[0])
        finish(stage, 2, sems[3])
    else:
        o[...] = s1[...]


def column_kernel(net, g, d1, tw, f2, m0, o, s1, r1, ure, uim, *sems):
    flat = s1.reshape(1024, 128) if net else s1
    cos, sin = tw[0], tw[1]
    for grp in range(8):
        x, at = [], []
        for i in (2 * grp, 2 * grp + 1):
            x += decode(g[pl.ds(i, 64, stride=16), :])
            at += [i, 16 + i]
        v = dot3(pair(d1), split(jnp.concatenate(x, 1)))
        for j in range(4):
            re = v[:32, j * 128 : (j + 1) * 128]
            im = v[32:, j * 128 : (j + 1) * 128]
            ure[pl.ds(at[j], 32, stride=32), :] = re * cos + im * sin
            uim[pl.ds(at[j], 32, stride=32), :] = im * cos - re * sin
    lane = lax.broadcasted_iota(jnp.int32, (256, 128), 1)

    def send(kg):
        if net and kg >= 0:
            to_col(kg, s1, r1, *sems[:3])
            to_col(kg + 4, s1, r1, *sems[:3])

    for kg in range(4):
        rows = slice(kg * 256, (kg + 1) * 256)
        rhs = split(jnp.concatenate([ure[rows, :], uim[rows, :]], 1))
        out = dot3(pair(f2), rhs, True)
        for h in range(2):
            part = out[:, h * 128 : (h + 1) * 128]
            if kg == 0 and h == 0:
                special = dot3(pair(m0), (rhs[0][:128], rhs[1][:128]), True)
                part = jnp.where(lane < 32, special, part)
            word = encode(part[:128], part[128:])
            for half in range(2):
                at = pl.ds((half * 4 + kg) * 128 + h, 64, stride=2)
                flat[at, :] = word[half * 64 : half * 64 + 64]
        send(kg - 1)
    send(3)
    if net:
        all_exchange(s1, r1, o, sems, True)
    else:
        o[...] = s1[...]


def column_wave(col):
    r, c = here()
    group = r * 2 + lax.div(c, 4)
    b = lax.rem(c, 4) * 8 + col + 64 * group
    if col == 0:
        b = b + jnp.where((lax.rem(c, 4) == 0) & (group >= 64), 32, 0)
    return jnp.where(b > N // 2, b - N, b).astype(F32) * (2.0 * math.pi / N)


def row_kernel(net, kb, x, e, tw, w2, ka_ref, w3, e4, o, s1, r1, uh, ul, sh, sl, yh, yl, *sems):
    flat = s1.reshape(512, 128) if net else s1
    for c in range(8):
        cos = jnp.concatenate([tw[0, c * 16 : c * 16 + 16, :]] * 8, 0)
        sin = jnp.concatenate([tw[1, c * 16 : c * 16 + 16, :]] * 8, 0)
        for h in range(2):
            block = jnp.concatenate(decode(x[pl.ds(c * 2 + h, 64, stride=16), :]), 0)
            both = dot3(split(block.T), pair(e))
            v, vs = both[:, :128], both[:, 128:]
            u = split(v * cos - vs * sin)
            us = split(vs * cos + v * sin)
            for kf in range(8):
                at = pl.ds((h * 8 + kf) * 128 + c * 16, 16)
                part = slice(kf * 16, kf * 16 + 16)
                uh[at, :] = u[0][part]
                ul[at, :] = u[1][part]
                sh[at, :] = us[0][part]
                sl[at, :] = us[1][part]
    ka = ka_ref[...]
    ka2 = ka * ka + FLOOR * FLOOR
    sign = jnp.where(lax.broadcasted_iota(jnp.int32, (128, 128), 1) < 64, -1.0, 1.0)

    def stack(first, second, col):
        parts = []
        for f in range(2):
            at = slice((col * 2 + f) * 128, (col * 2 + f + 1) * 128)
            parts.append(jnp.concatenate([first[at, :], second[at, :]], 0))
        return jnp.concatenate(parts, 1)

    for pr in range(4):
        q, qs = [], []
        for j in range(2):
            col = pr * 2 + j
            out = dot3(pair(w2), (stack(uh, sh, col), stack(ul, sl, col)))
            wb = column_wave(col) if net else kb[col]
            weight = LOCAL_WEIGHT + 1.0 / (ka2 + wb * wb)
            mixed = weight * (wb * out[:, :128] + ka * out[:, 128:])
            q.append(mixed)
            qs.append(pltpu.roll(mixed, 64, 1) * sign)
        rhs = jnp.concatenate([jnp.concatenate(q, 1), jnp.concatenate(qs, 1)], 0)
        back = dot3(pair(w3), split(rhs))
        for j in range(2):
            col = pr * 2 + j
            b = back[:128, j * 128 : (j + 1) * 128]
            bs = back[128:, j * 128 : (j + 1) * 128]
            y = split(b * tw[0] + bs * tw[1])
            for c in range(8):
                at = pl.ds(c * 128 + col * 16, 16)
                yh[at, :] = y[0][c * 16 : c * 16 + 16]
                yl[at, :] = y[1][c * 16 : c * 16 + 16]
    for c in range(8):
        rows = slice(c * 128, (c + 1) * 128)
        out = dot3(pair(e4), (yh[rows, :], yl[rows, :]), True)
        flat[c * 64 : c * 64 + 64, :] = encode(out[:64], out[64:])
        if net and c > 0:
            to_col(c - 1, s1, r1, *sems[:3])
    if net:
        to_col(COLS - 1, s1, r1, *sems[:3])
        all_exchange(s1, r1, o, sems, False)
    else:
        o[...] = s1[...]


def image_kernel(net, t, f4, m0i, tw, d4, o, s1, r1, vre, vim, *sems):

    flat = s1.reshape(512, 128) if net else s1
    for kg in range(4):
        block = decode(t[pl.ds(kg, 128, stride=4), :])
        lhs = split(jnp.concatenate([part.T for part in block], 1))
        v = dot3(lhs, pair(f4))
        if kg == 0:
            special = dot3((lhs[0][:16], lhs[1][:16]), pair(m0i))
            v = jnp.concatenate([special, v[16:]], 0)
        for col in range(8):
            kk = kg * 8 + col
            re = v[col * 16 : col * 16 + 16, :128]
            im = v[col * 16 : col * 16 + 16, 128:]
            cos = tw[0, kk : kk + 1, :]
            sin = tw[1, kk : kk + 1, :]
            vre[kk * 16 : kk * 16 + 16, :] = re * cos - im * sin
            vim[kk * 16 : kk * 16 + 16, :] = im * cos + re * sin
    for grp in range(4):
        picks = (grp * 2, grp * 2 + 8, grp * 2 + 1, grp * 2 + 9)
        cols = []
        for i in picks:
            at = pl.ds(i, 32, stride=16)
            cols.append(jnp.concatenate([vre[at, :], vim[at, :]], 0))
        out = dot3(pair(d4), split(jnp.concatenate(cols, 1)))
        for j in range(2):
            word = encode(out[:, j * 256 : j * 256 + 128], out[:, j * 256 + 128 : j * 256 + 256])
            flat[pl.ds(grp * 2 + j, 64, stride=8), :] = word
    if net:
        own = here()[1]
        for i in range(1, COLS):
            to_col(lax.rem(own + i, COLS), s1, r1, *sems)
        r1[own] = s1[own]
        finish(r1, 3, sems[1])
        finish(r1, 4, sems[2])
    else:
        r1[...] = s1[...]
    for c in range(8):
        halves = decode(r1[c] if net else r1[c * 64 : c * 64 + 64, :])
        for it in range(2):
            for ph in range(8):
                at = slice(c * 16 + it * 8, c * 16 + it * 8 + 8)
                o[at, ph * 128 : ph * 128 + 128] = halves[it][ph * 8 : ph * 8 + 8]
    if net:
        finish(s1, COLS - 1, sems[0])


INPUTS = 19


def whole_kernel(*refs):
    inputs, out, rest = refs[:INPUTS], refs[INPUTS], refs[INPUTS + 1 :]
    held, scratch, sems = rest[:INPUTS], rest[INPUTS:-20], rest[-20:-1]
    flow_land, s_flow, spec_land, s_spec, r_spec, mix_land, s_mix, r_mix, s_img, r_img = scratch[:10]
    padded, spots, wts, sc, ure, uim, uh, ul, sh, sl, yh, yl, vre, vim, stage, land = scratch[10:]
    x, slopes, tile, rshift, pshift, frac, d1, tw1, f2, m0, e, tw2, w2, ka, w3, e4, f4, m0i, d4 = held
    greet()
    loads = [
        pltpu.make_async_copy(inputs[i], held[i], rest[-1].at[i]) for i in range(INPUTS)
    ]
    for load in loads:
        load.start()
    for load in loads[:6]:
        load.wait()
    pull_kernel(
        True, x, None, None, slopes, tile, rshift, pshift, frac,
        flow_land, s_flow, padded, spots, wts, sc, stage, land, *sems[:3], *sems[16:],
    )
    for load in loads[6:]:
        load.wait()
    column_kernel(
        True, flow_land.reshape(1024, 128), d1, tw1, f2, m0,
        spec_land, s_spec, r_spec, ure, uim, *sems[3:8],
    )
    row_kernel(
        True, None, spec_land.reshape(1024, 128), e, tw2, w2, ka, w3, e4,
        mix_land, s_mix, r_mix, uh, ul, sh, sl, yh, yl, *sems[8:13],
    )
    image_kernel(
        True, mix_land.reshape(512, 128), f4, m0i, tw1, d4,
        out, s_img, r_img, vre, vim, *sems[13:16],
    )


def call(kernel, out, scratch, *args, net=None, phases=1, smem=()):
    specs = [
        pl.BlockSpec(memory_space=pltpu.SMEM if i in smem else pltpu.VMEM)
        for i in range(len(args))
    ]
    params = {}
    if net is not None:
        scratch = scratch + [pltpu.SemaphoreType.DMA] * (2 * phases)
        params["compiler_params"] = pltpu.CompilerParams(collective_id=net, has_side_effects=True)
    return pl.pallas_call(
        functools.partial(kernel, net is not None),
        out_shape=jax.ShapeDtypeStruct(*out),
        in_specs=specs,
        out_specs=pl.BlockSpec(memory_space=pltpu.VMEM),
        scratch_shapes=scratch,
        **params,
    )(*args)


def two(table):
    return jnp.asarray(np.stack(table))


def words(*shape):
    return pltpu.VMEM(shape, jnp.int32)


def pull(x, before, after, slopes, tile, rshift, pshift, frac, net=None):
    flip = lambda y: jnp.transpose(y, (0, 2, 1))
    return call(
        pull_kernel,
        ((8, 128, 128), jnp.int32),
        [
            words(8, 128, 128),
            pltpu.VMEM((2, 144, 1024), F32),
            pltpu.VMEM((16, 128), jnp.int32),
            pltpu.VMEM((6, 16, 128), F32),
            pltpu.VMEM((2, 2, 144, 128), F32),
        ],
        x, before, after, slopes, flip(tile), flip(rshift), flip(pshift), flip(frac),
        net=net,
    )


def column_transform(g, net=None):
    t = tables()
    return call(
        column_kernel,
        ((64, 8, 2, 128) if net is not None else (1024, 128), jnp.int32),
        [words(8, 64, 2, 128) if net is not None else words(1024, 128)] * 2 + [pltpu.VMEM((1024, 128), F32)] * 2,
        g, two(t["d1"]), jnp.asarray(t["tw1"]), two(t["f2"]), two(t["m0"]),
        net=net, phases=2,
    )


def row_transform(x, device, net=None):
    t = tables()
    group, low = device // 4, device % 4
    kk = low * 8 + jnp.arange(8, dtype=jnp.int32)
    b = kk + 64 * group + jnp.where((kk == 0) & (group >= 64), 32, 0)
    kb = jnp.where(b > N // 2, b - N, b).astype(F32) * (2.0 * math.pi / N)
    return call(
        row_kernel,
        ((64, 8, 1, 128) if net is not None else (512, 128), jnp.int32),
        [words(8, 64, 1, 128) if net is not None else words(512, 128)] * 2
        + [pltpu.VMEM((2048, 128), BF16)] * 4
        + [pltpu.VMEM((1024, 128), BF16)] * 2,
        kb, x, two(t["e"]), jnp.asarray(t["tw2"]), two(t["w2"]), jnp.asarray(t["ka"]),
        two(t["w3"]), two(t["e4"]),
        smem=(0,), net=net, phases=2,
    )


def image_transform(y, net=None):
    t = tables()
    return call(
        image_kernel,
        ((128, 1024), F32),
        [words(8, 64, 128) if net is not None else words(512, 128)] * 2 + [pltpu.VMEM((512, 128), F32)] * 2,
        y, two(t["f4"]), two(t["m0i"]), jnp.asarray(t["tw1"]), two(t["d4"]),
        net=net,
    )


def per_device(residual, field_slopes, source_tile, row_shift, pixel_shift, fraction):
    flip = lambda y: jnp.transpose(y, (0, 2, 1))
    t = tables()
    plain = lambda name: jnp.asarray(t[name])
    args = (
        residual, field_slopes,
        flip(source_tile), flip(row_shift), flip(pixel_shift), flip(fraction),
        two(t["d1"]), plain("tw1"), two(t["f2"]), two(t["m0"]), two(t["e"]), plain("tw2"),
        two(t["w2"]), plain("ka"), two(t["w3"]), two(t["e4"]), two(t["f4"]), two(t["m0i"]),
        two(t["d4"]),
    )
    f32 = lambda *shape: pltpu.VMEM(shape, F32)
    bf16 = lambda *shape: pltpu.VMEM(shape, BF16)
    scratch = (
        [pltpu.VMEM(a.shape, a.dtype) for a in args]
        + [words(8, 128, 128)] * 2
        + [words(64, 8, 2, 128)] + [words(8, 64, 2, 128)] * 2
        + [words(64, 8, 1, 128)] + [words(8, 64, 1, 128)] * 2
        + [words(8, 64, 128)] * 2
        + [f32(2, 144, 1024), words(16, 128), f32(6, 16, 128), f32(2, 2, 144, 128)]
        + [f32(1024, 128)] * 2
        + [bf16(2048, 128)] * 4 + [bf16(1024, 128)] * 2
        + [f32(512, 128)] * 2
        + [bf16(2, 2, 8, 1024)] * 2
        + [pltpu.SemaphoreType.DMA] * 19
        + [pltpu.SemaphoreType.DMA((INPUTS,))]
    )
    return pl.pallas_call(
        whole_kernel,
        out_shape=pltpu.VMEM((128, 1024), F32),
        in_specs=[pl.BlockSpec(memory_space=pl.ANY)] * len(args),
        out_specs=pl.BlockSpec(memory_space=pltpu.VMEM),
        scratch_shapes=scratch,
        compiler_params=pltpu.CompilerParams(collective_id=0, has_side_effects=True),
    )(*args)


def solution(mesh):
    spec = P(None, "rows", "cols")
    return jax.shard_map(
        per_device,
        mesh=mesh,
        in_specs=(spec,) * 6,
        out_specs=P("rows", "cols"),
        check_vma=False,
    )
```
